512 devices in a mesh: rows: 128 (over y, z, core), feat: 4 (over x).
Axes of the slice: x: 4, y: 8, z: 8, core: 2. Of those that a mesh axis runs over, the one named last changes fastest.
Arguments:
- features: bfloat16 [1048576, 1024], P('rows', 'feat'), may hold values from -6 to 6
- gradients: float32 [1048576], P(('rows', 'feat')), may hold values from -2.7 to 2.7
- hessians: float32 [1048576], P(('rows', 'feat')), may hold values from 0.05 to 0.75
- node_ids: int32 [1048576], P('rows'), may hold values from 0 to 3
- sample_flags: int32 [1048576], P('rows'), may hold values 0 or 1
- kept_index: int32 [524288], P('rows'), may hold values from 0 to 8191, as said below
- kept_count: int32 [128], P('rows'), may hold values from 1 to 4096, 131072 in all
- cut_edges: int32 [1024, 128], P('feat'), may hold values from 0 to 128
Outputs:
- split_gain: float32 [1024, 4, 128], P(('feat', 'rows'))
- cut_rank: float32 [1024, 4, 128], P(('feat', 'rows'))
The draws below stay inside these ranges and needn't reach their ends.
Inputs may be any that keep to these rules, and one draw needn't show every extreme that they name: `kept_index`: within the 4096 entries of one index of rows the numbers are distinct local row numbers; entries at slot kept_count of that index or later are not used. `kept_count`: one count for each index of rows; the counts sum to exactly 131072, and the largest is exactly 4096.
All inputs are finite; a program needn't handle non-finite values. No bound on the sum of `sample_flags` on one device may be relied on, other than what follows from the above.
Results may differ from the reference program's by a relative error of at most 0.007.
Values may be sent and summed in bfloat16 or wider, within the bound.
A program may use at most 64 MiB of HBM per device.

```python
import math
import jax
import jax.numpy as jnp
import numpy as np
from jax import lax

F = 1024
CUTS = 128
NODES = 4
SHARE = 1024
ROWS_DEV = 8192
KEEP_MAX = 4096
GROUPS = 128
ROWS = 1048576


def draw_gradients(key, part):
    row_ramp = 1.0 + 2.0 * jnp.arange(ROWS, dtype=jnp.float32) / ROWS
    values = 0.3 * jnp.clip(jax.random.normal(key, (ROWS,), jnp.float32), -3.0, 3.0) * row_ramp
    return values.astype(jnp.float32)


def draw_hessians(key, part):
    row_ramp = 1.0 + 2.0 * jnp.arange(ROWS, dtype=jnp.float32) / ROWS
    values = jax.random.uniform(key, (ROWS,), jnp.float32, 0.05, 0.25) * row_ramp
    return values.astype(jnp.float32)


def draw_kept_index(key, part):
    group_count = ROWS // ROWS_DEV
    group_keys = jax.random.split(key, group_count)

    def one_group(group_key):
        return jax.random.permutation(group_key, ROWS_DEV)[:KEEP_MAX]
    picked = jax.vmap(one_group)(group_keys)
    return picked.reshape(group_count * KEEP_MAX).astype(jnp.int32)


def touch_ends(values, rng, low, largest):
    longest = values.shape.index(max(values.shape))
    spots = []
    for shift in (0, 1):
        where = [jax.random.randint(jax.random.fold_in(rng, axis), (), 0, length) for axis, length in enumerate(values.shape)]
        where[longest] = (where[longest] + shift) % values.shape[longest]
        spots.append(tuple(where))
    return values.at[spots[0]].set(low).at[spots[1]].set(largest)


def level_of(rng, dims, cuts, smallest, high):
    level, own = 1.0, jax.random.fold_in(rng, 6)
    for dim, shards_of in cuts:
        draws = jnp.exp(jax.random.uniform(jax.random.fold_in(own, dim), (shards_of,), jnp.float32, smallest / len(cuts), high / len(cuts)))
        level = level * jnp.repeat(draws, dims[dim] // shards_of).reshape([-1 if axis == dim else 1 for axis in range(len(dims))])
    return level


def split_up(amount, total, reach, skew):
    portions = [(1 << 20) // math.isqrt(grade ** skew) + 1 for grade in range(2, amount + 1)]
    rest, given = total - reach - (amount - 1), [1] * (amount - 1)
    while rest > 0:
        free = [i for i in range(amount - 1) if given[i] < reach]
        pool, remaining = sum([portions[i] for i in free]), rest
        for i in free:
            more = min(reach - given[i], max(1, remaining * portions[i] // pool), rest)
            given[i] = given[i] + more
            rest = rest - more
    return np.array([reach] + given)


def uneven(rng, amount, total, limit, skew):
    if amount == 2:
        one = jax.random.randint(rng, (), max(1, total - limit), min(limit, total - 1) + 1)
        return jnp.stack([one, total - one])
    tallies = jnp.asarray(split_up(amount, total, limit, skew), jnp.int32)
    twos = (amount - 1) // 2
    source_of, sink = tallies[1:1 + 2 * twos:2], tallies[2:2 + 2 * twos:2]
    slack = jnp.minimum(source_of - 1, limit - sink)
    shifted = jax.random.randint(jax.random.fold_in(rng, 1), (twos,), 0, 1 << 20) % (slack + 1)
    tallies = tallies.at[1:1 + 2 * twos:2].set(source_of - shifted).at[2:2 + 2 * twos:2].set(sink + shifted)
    return tallies[jax.random.permutation(jax.random.fold_in(rng, 2), amount)]


def scatter_about(rng, shape, deviation, reach, pieces=(), kind=jnp.bfloat16):
    level = level_of(rng, shape, pieces, -0.22, 0.18) if pieces else 1.0
    entries = jax.random.normal(rng, shape, jnp.float32) * deviation * level
    return jnp.minimum(jnp.maximum(entries, -reach), reach).astype(kind)


def setup_inputs(seed: int = 0) -> dict:
    key_of = jax.random.split(jax.random.key(seed), 9)
    return {
        "features": scatter_about(key_of[0], (ROWS, F), 1.5, 6.0, ((0, 128), (1, 4))),
        "gradients": draw_gradients(jax.random.fold_in(key_of[8], 71), 0),
        "hessians": draw_hessians(jax.random.fold_in(key_of[8], 71), 0),
        "node_ids": touch_ends(jax.random.randint(key_of[3], (ROWS,), 0, NODES), jax.random.fold_in(key_of[3], 1), 0, NODES - 1).astype(jnp.int32),
        "sample_flags": touch_ends((jax.random.randint(key_of[4], (ROWS,), 0, 3) < 1).astype(jnp.int32), jax.random.fold_in(key_of[4], 1), 0, 1),
        "kept_index": draw_kept_index(jax.random.fold_in(key_of[8], 71), 0),
        "kept_count": uneven(key_of[6], GROUPS, GROUPS * SHARE, KEEP_MAX, 2).astype(jnp.int32),
        "cut_edges": touch_ends(jax.random.randint(key_of[7], (F, CUTS), 0, 129), jax.random.fold_in(key_of[7], 1), 0, 128).astype(jnp.int32),
    }


amplify_factor = 8.0
regularize = 1.0
edge_step = 0.0625
edge_anchor = 4.0


def histogram(kept_columns, kept_weights, cut_values):
    feature_count, slot_count = kept_columns.shape
    feature_width = math.gcd(feature_count, 16)
    slot_width = math.gcd(slot_count, 1024)
    weight_rows = kept_weights.shape[0]
    cut_count = cut_values.shape[1]

    def feature_block(i):
        block_rows = lax.dynamic_slice_in_dim(kept_columns, i * feature_width, feature_width, 0)
        block_cuts = lax.dynamic_slice_in_dim(cut_values, i * feature_width, feature_width, 0)

        def add_slots(j, running):
            slot_part = lax.dynamic_slice_in_dim(block_rows, j * slot_width, slot_width, 1)
            weight_part = lax.dynamic_slice_in_dim(kept_weights, j * slot_width, slot_width, 1)
            compare = (slot_part.astype(jnp.float32)[:, None, :] <= block_cuts[:, :, None]).astype(jnp.bfloat16)
            compare = compare.reshape(feature_width * cut_count, slot_width)
            return running + lax.dot_general(weight_part, compare, (((1,), (1,)), ((), ())), preferred_element_type=jnp.float32)

        start_value = jnp.zeros((weight_rows, feature_width * cut_count), jnp.float32)
        running = lax.fori_loop(0, slot_count // slot_width, add_slots, start_value)
        return running.reshape(weight_rows, feature_width, cut_count).transpose(1, 0, 2)

    blocks = lax.map(feature_block, jnp.arange(feature_count // feature_width, dtype=jnp.int32))
    return blocks.reshape(feature_count, weight_rows, cut_count)


def split_gains(node_hist, totals, node_count):
    grad_left = node_hist[:, :node_count]
    hess_left = node_hist[:, node_count:]
    grad_sum = totals[:node_count][None, :, None]
    hess_sum = totals[node_count:][None, :, None]
    split_gain = grad_left * grad_left / (hess_left + regularize) + (grad_sum - grad_left) ** 2 / (hess_sum - hess_left + regularize) - grad_sum * grad_sum / (hess_sum + regularize)
    cut_rank = hess_left / hess_sum
    return split_gain, cut_rank


def reference(features, gradients, hessians, node_ids, sample_flags, kept_index, kept_count, cut_edges):
    group_count = kept_count.shape[0]
    live_total = group_count * SHARE
    count_ends = jnp.cumsum(kept_count).astype(jnp.int32)
    count_starts = (count_ends - kept_count).astype(jnp.int32)
    live_order = jnp.arange(live_total, dtype=jnp.int32)
    owner_group = jnp.searchsorted(count_ends, live_order, side="right").astype(jnp.int32)
    within = (live_order - count_starts[owner_group]).astype(jnp.int32)
    local_row = kept_index[(owner_group * KEEP_MAX + within).astype(jnp.int32)]
    kept_rows = (owner_group * ROWS_DEV + local_row).astype(jnp.int32)
    factor = jnp.where(sample_flags[kept_rows] == 1, jnp.float32(amplify_factor), jnp.float32(1.0))
    grad_weight = (gradients[kept_rows] * factor).astype(jnp.bfloat16)
    hess_weight = (hessians[kept_rows] * factor).astype(jnp.bfloat16)
    node_of = node_ids[kept_rows]
    onehot = jnp.arange(NODES, dtype=jnp.int32)[:, None] == node_of[None, :]
    zero_value = jnp.zeros((), jnp.bfloat16)
    kept_weights = jnp.concatenate([jnp.where(onehot, grad_weight[None, :], zero_value), jnp.where(onehot, hess_weight[None, :], zero_value)], axis=0)
    kept_columns = features[kept_rows].T
    cut_values = cut_edges.astype(jnp.float32) * edge_step - edge_anchor
    node_hist = histogram(kept_columns, kept_weights, cut_values)
    totals = jnp.sum(kept_weights.astype(jnp.float32), axis=1)
    return split_gains(node_hist, totals, NODES)
```

```python
import functools

import jax
import jax.numpy as jnp
from jax import lax
from jax.experimental import pallas as pl
from jax.experimental.pallas import tpu as pltpu
from jax.sharding import PartitionSpec as P

MESH = pl.DeviceIdType.MESH
NODES = 4
BLOCK = 256
WIN = 64
NT = (((1,), (1,)), ((), ()))
VM = pl.BlockSpec(memory_space=pltpu.VMEM)
SM = pl.BlockSpec(memory_space=pltpu.SMEM)
HBM = pl.BlockSpec(memory_space=pl.ANY)
F32, BF16, I32 = jnp.float32, jnp.bfloat16, jnp.int32


def iota(shape, dim, kind=I32):
    return lax.broadcasted_iota(I32, shape, dim).astype(kind)


def onehot(cond):
    return jnp.where(cond, 1.0, 0.0).astype(BF16)


def share_body(peers, g_ref, h_ref, out_ref, send_sem, recv_sem):
    row, me = lax.axis_index("rows"), lax.axis_index("feat")
    barrier = pltpu.get_barrier_semaphore()
    for d in range(1, peers):
        pl.semaphore_signal(barrier, inc=1, device_id=(row, lax.rem(me + d, peers)), device_id_type=MESH)
    out_ref[me, 0] = g_ref[...]
    out_ref[me, 1] = h_ref[...]
    pl.semaphore_wait(barrier, peers - 1)
    copies = []
    for d in range(1, peers):
        to = (row, lax.rem(me + d, peers))
        for w, ref in enumerate((g_ref, h_ref)):
            copies.append(
                pltpu.make_async_remote_copy(
                    src_ref=ref,
                    dst_ref=out_ref.at[me, w],
                    send_sem=send_sem.at[d, w],
                    recv_sem=recv_sem.at[d, w],
                    device_id=to,
                    device_id_type=MESH,
                )
            )
    for c in copies:
        c.start()
    for c in copies:
        c.wait()


def share(gradients, hessians, peers):
    part = gradients.shape[0]
    return pl.pallas_call(
        functools.partial(share_body, peers),
        out_shape=jax.ShapeDtypeStruct((peers, 2, part // 128, 128), F32),
        in_specs=[VM, VM],
        out_specs=VM,
        scratch_shapes=[pltpu.SemaphoreType.DMA((peers, 2)), pltpu.SemaphoreType.DMA((peers, 2))],
        compiler_params=pltpu.CompilerParams(collective_id=0, has_side_effects=True),
        name="share",
    )(gradients.reshape(part // 128, 128), hessians.reshape(part // 128, 128))


def hist_body(
    cnt_s, feat, idx_v, gh, node_v, flag_v, main, extra,
    xb, xs, ws, pos, tpose, hi_s, lo_s, w16_s, acc, exacc, totacc, offs_v, offs_s, ext, sem, osem,
):
    rows, width = feat.shape
    lines = rows // 128
    slots = idx_v.shape[1]
    chunks = 8
    per = rows // chunks

    def load(i):
        return pltpu.make_async_copy(feat.at[pl.ds(i * per, per)], xb.at[pl.ds(i * per, per)], sem.at[i])

    for i in range(chunks):
        load(i).start()
    count = cnt_s[0]

    kept = jnp.zeros((lines, 128), F32)
    for q in range(slots // 1024):
        ids = idx_v[:, pl.ds(q * 1024, 1024)]
        ids = jnp.where(iota((1, 1024), 1) + q * 1024 < count, ids, -1)
        upper = onehot(iota((lines, 1024), 0) == (ids >> 7))
        lower = onehot(iota((128, 1024), 0) == (ids & 127))
        kept += lax.dot_general(upper, lower, NT, preferred_element_type=F32)

    before = onehot(iota((128, 128), 0) < iota((128, 128), 1))
    above = onehot(iota((lines, lines), 1) < iota((lines, lines), 0))
    upto = onehot(iota((lines, 128), 0) < iota((lines, 128), 1))
    ranks = []
    for k in range(NODES):
        mine = (kept > 0.5) & (node_v[...] == k)
        ones = onehot(mine)
        per_line = jnp.sum(jnp.where(mine, 1.0, 0.0), axis=1, keepdims=True)
        rank = jnp.dot(ones, before, preferred_element_type=F32)
        rank += jnp.dot(above, jnp.broadcast_to(per_line, (lines, 128)).astype(BF16), preferred_element_type=F32)
        ranks.append((mine, rank))
        counts = lax.dot_general(jnp.ones((8, 128), BF16), ones, NT, preferred_element_type=F32)
        starts = jnp.dot(counts.astype(BF16), upto, preferred_element_type=F32)
        offs_v[pl.ds(k, 1), :] = starts[0:1].astype(I32)
    to_scalar = pltpu.make_async_copy(offs_v, offs_s, osem)
    to_scalar.start()

    factor = jnp.where(flag_v[...] == 1, 8.0, 1.0)
    grad = gh[:, 0].reshape(lines, 128) * factor
    hess = gh[:, 1].reshape(lines, 128) * factor
    tpose[...] = jnp.concatenate([grad, hess], axis=0).astype(BF16).astype(F32).T.astype(BF16)

    def clear(t, _):
        z = pl.multiple_of(t * 256, 256)
        xs[pl.ds(z, 256), :] = jnp.zeros((256, width), F32)
        ws[pl.ds(z, 256), :] = jnp.zeros((256, 128), F32)
        return 0

    lax.fori_loop(0, xs.shape[0] // 256, clear, 0)
    acc[...] = jnp.zeros_like(acc)
    exacc[...] = jnp.zeros_like(exacc)
    totacc[...] = jnp.zeros_like(totacc)
    to_scalar.wait()
    sizes = [offs_s[k, lines] for k in range(NODES)]
    bases, blocks = [], []
    base = jnp.int32(0)
    for k in range(NODES):
        bases.append(base)
        blocks.append((sizes[k] + (BLOCK - 1)) // BLOCK)
        base = base + blocks[k] * BLOCK
        mine, rank = ranks[k]
        pos[k] = jnp.where(mine, rank + bases[k].astype(F32), -1.0)

    for i in range(chunks):
        load(i).wait()

    place = iota((WIN, 256), 0).astype(F32).astype(BF16)
    lane = iota((128, 128), 1) & (lines - 1)

    def compact(t, _):
        r0 = pl.multiple_of(t * 256, 256)
        x = xb[pl.ds(r0, 256), :]
        tp = tpose[...]
        zero = jnp.zeros((), BF16)
        wn = jnp.concatenate([jnp.where(lane == 2 * t, tp, zero), jnp.where(lane == 2 * t + 1, tp, zero)], axis=0)
        first, trips = [], jnp.int32(0)
        for k in range(NODES):
            start = bases[k] + offs_s[k, 2 * t]
            stop = bases[k] + offs_s[k, 2 * t + 2]
            a = (start >> 3) << 3
            first.append(a)
            trips = jnp.maximum(trips, jnp.where(stop > start, (stop - a + (WIN - 1)) // WIN, 0))
        prs = [jnp.concatenate([pos[k, pl.ds(2 * t, 1), :], pos[k, pl.ds(2 * t + 1, 1), :]], axis=1) for k in range(NODES)]

        def window(i, _):
            picks = []
            for k in range(NODES):
                d = prs[k] - (first[k] + WIN * i).astype(F32)
                d = jnp.where((d >= 0) & (d < WIN), d, -1.0)
                d = jnp.broadcast_to(d, (WIN, 256)).astype(BF16)
                picks.append(jnp.where(d == place, jnp.ones((), BF16), zero))
            pick = jnp.concatenate(picks, axis=0)
            got = jnp.dot(pick, x, preferred_element_type=F32)
            gotw = jnp.dot(pick, wn, preferred_element_type=F32)
            for k in range(NODES):
                at = pl.ds(pl.multiple_of(first[k] + WIN * i, 8), WIN)
                xs[at, :] += got[k * WIN:(k + 1) * WIN]
                ws[at, :] += gotw[k * WIN:(k + 1) * WIN]
            return 0

        lax.fori_loop(0, trips, window, 0)
        return 0

    lax.fori_loop(0, rows // 256, compact, 0)

    sum_kind = onehot((iota((16, 128), 0) >> 3) == (iota((16, 128), 1) >> 6))
    his = (iota((16, BLOCK), 0) & 7).astype(F32).astype(BF16)
    ramp = (iota((16, BLOCK), 0) + 1).astype(F32).astype(BF16)
    owner = iota((16, 256), 1) >> 4

    def node_loop(k, _):
        base = jnp.where(k == 0, bases[0], jnp.where(k == 1, bases[1], jnp.where(k == 2, bases[2], bases[3])))
        trips = jnp.where(k == 0, blocks[0], jnp.where(k == 1, blocks[1], jnp.where(k == 2, blocks[2], blocks[3])))

        def block(q, _):
            s = pl.multiple_of(base + q * BLOCK, BLOCK)
            x = xs[pl.ds(s, BLOCK), :]
            w16 = lax.dot_general(sum_kind, ws[pl.ds(s, BLOCK), :].astype(BF16), NT, preferred_element_type=F32)
            w16b = w16.astype(BF16)
            w16_s[...] = w16b
            totacc[k] += w16
            exacc[k] += jnp.dot(w16b, onehot(x <= 4.0), preferred_element_type=F32)
            cat = jnp.maximum(jnp.ceil(x.T * 16.0) + 64.0, 0.0)
            hi = jnp.floor(cat * 0.0625)
            hi_s[...] = hi
            lo_s[...] = cat - hi * 16.0 + 1.0

            def group(g, _):
                w16v = w16_s[...]
                f0 = (g >> 1) * 32 + (g & 1)
                a, b = [], []
                for f in range(16):
                    hb = jnp.broadcast_to(hi_s[pl.ds(f0 + 2 * f, 1), :], (16, BLOCK)).astype(BF16)
                    lb = jnp.broadcast_to(lo_s[pl.ds(f0 + 2 * f, 1), :], (16, BLOCK)).astype(BF16)
                    a.append(jnp.where(hb == his, w16v, jnp.zeros((), BF16)))
                    b.append(jnp.minimum(lb, ramp))
                r = lax.dot_general(
                    jnp.concatenate(a, axis=0), jnp.concatenate(b, axis=0), NT, preferred_element_type=F32
                )
                mine = r[0:16]
                for f in range(1, 16):
                    mine = jnp.where(owner == f, r[16 * f:16 * f + 16], mine)
                acc[k, g] += mine
                return 0

            lax.fori_loop(0, width // 16, group, 0, unroll=2)
            return 0

        lax.fori_loop(0, trips, block, 0)
        return 0

    lax.fori_loop(0, NODES, node_loop, 0)

    for j in range(width // 32):
        parts = [acc[k, 2 * j + half, 8 * w:8 * w + 8, :] for half in range(2) for w in range(2) for k in range(NODES)]
        t = jnp.concatenate(parts, axis=0).T
        for z in range(8):
            for c in range(2):
                main[c, z, j] = t[(2 * z + c) * 16:(2 * z + c) * 16 + 16]
    whole = [jnp.sum(totacc[k], axis=1, keepdims=True) for k in range(NODES)]
    lines_ex = [exacc[k, 8 * w:8 * w + 1, :] for w in range(2) for k in range(NODES)]
    lines_ex += [jnp.broadcast_to(whole[k][8 * w:8 * w + 1], (1, width)) for w in range(2) for k in range(NODES)]
    lines_ex.append(jnp.zeros((112, width), F32))
    ext[...] = jnp.concatenate(lines_ex, axis=0).T
    even, odd = ext[pl.ds(0, width // 2, stride=2), :], ext[pl.ds(1, width // 2, stride=2), :]
    both = even + pltpu.roll(odd, 16, 1)
    for j in range(8):
        for z in range(8):
            for c in range(2):
                p = j * 16 + z * 2 + c
                extra[c, z, j] = both[p:p + 1]


def local_histogram(kept_count, features, kept_index, gh, node_ids, sample_flags):
    rows, width = features.shape
    slots = kept_index.shape[0]
    lines = rows // 128
    room = slots + NODES * BLOCK + 512
    return pl.pallas_call(
        hist_body,
        out_shape=(
            jax.ShapeDtypeStruct((2, 8, 8, 16, 128), F32),
            jax.ShapeDtypeStruct((2, 8, 8, 1, 128), F32),
        ),
        in_specs=[SM, HBM, VM, VM, VM, VM],
        out_specs=(VM, VM),
        scratch_shapes=[
            pltpu.VMEM((rows, width), BF16),
            pltpu.VMEM((room, width), F32),
            pltpu.VMEM((room, 128), F32),
            pltpu.VMEM((NODES, lines, 128), F32),
            pltpu.VMEM((128, 128), BF16),
            pltpu.VMEM((width, BLOCK), F32),
            pltpu.VMEM((width, BLOCK), F32),
            pltpu.VMEM((16, BLOCK), BF16),
            pltpu.VMEM((NODES, width // 16, 16, 256), F32),
            pltpu.VMEM((NODES, 16, width), F32),
            pltpu.VMEM((NODES, 16, BLOCK), F32),
            pltpu.VMEM((8, 128), I32),
            pltpu.SMEM((8, 128), I32),
            pltpu.VMEM((width, 128), F32),
            pltpu.SemaphoreType.DMA((8,)),
            pltpu.SemaphoreType.DMA,
        ],
        compiler_params=pltpu.CompilerParams(vmem_limit_bytes=56 << 20),
        name="local_histogram",
    )(
        kept_count,
        features,
        kept_index.reshape(1, slots),
        gh,
        node_ids.reshape(lines, 128),
        sample_flags.reshape(lines, 128),
    )


def gain_body(
    main, extra, edges, gain, rank,
    c1, e1, s1, t1, c2, e2, s2, t2, c3, e3,
    sem1, sem2, sem3,
):
    row, feat = lax.axis_index("rows"), lax.axis_index("feat")
    core, z, y = lax.rem(row, 2), lax.rem(row // 2, 8), row // 16

    def at(yy, zz, cc):
        return (yy * 16 + zz * 2 + cc, feat)

    barrier = pltpu.get_barrier_semaphore()
    pl.semaphore_signal(barrier, inc=1, device_id=at(y, z, 1 - core), device_id_type=MESH)
    for d in range(1, 8):
        pl.semaphore_signal(barrier, inc=1, device_id=at(y, lax.rem(z + d, 8), core), device_id_type=MESH)
        pl.semaphore_signal(barrier, inc=1, device_id=at(lax.rem(y + d, 8), z, core), device_id_type=MESH)
    pl.semaphore_wait(barrier, 15)

    def copy(src, dst, sems, i, w, to):
        return pltpu.make_async_remote_copy(
            src_ref=src, dst_ref=dst, send_sem=sems.at[0, i, w], recv_sem=sems.at[1, i, w],
            device_id=to, device_id_type=MESH,
        )

    other = at(y, z, 1 - core)
    pair = [copy(main.at[1 - core], c1, sem1, 0, 0, other), copy(extra.at[1 - core], e1, sem1, 0, 1, other)]
    for c in pair:
        c.start()
    for c in pair:
        c.wait()

    def add1(i, _):
        s1[i] = main[core, i] + c1[i]
        t1[i] = extra[core, i] + e1[i]
        return 0

    lax.fori_loop(0, 8, add1, 0)

    sends = []
    for d in range(1, 8):
        zz = lax.rem(z + d, 8)
        to = at(y, zz, core)
        sends.append(copy(s1.at[zz], c2.at[d - 1], sem2, d - 1, 0, to))
        sends.append(copy(t1.at[zz], e2.at[d - 1], sem2, d - 1, 1, to))
    for c in sends:
        c.start()
    for c in sends:
        c.wait()

    def add2(i, _):
        a, b = s1[z, i], t1[z, i]
        for d in range(7):
            a += c2[d, i]
            b += e2[d, i]
        s2[i] = a
        t2[i] = b
        return 0

    lax.fori_loop(0, 8, add2, 0)

    sends = []
    for d in range(1, 8):
        yy = lax.rem(y + d, 8)
        to = at(yy, z, core)
        sends.append(copy(s2.at[yy], c3.at[d - 1], sem3, d - 1, 0, to))
        sends.append(copy(t2.at[yy], e3.at[d - 1], sem3, d - 1, 1, to))
    for c in sends:
        c.start()
    for c in sends:
        c.wait()
    a, b = s2[y], t2[y]
    for d in range(7):
        a += c3[d]
        b += e3[d]

    line = iota((16, 128), 0)
    rest = a - jnp.where(line == 0, 0.0, pltpu.roll(a, 1, 0))
    bins = rest - jnp.where(line == 15, 0.0, pltpu.roll(rest, 15, 0))
    hi = iota((16, 128), 1) & 7
    spread = jnp.concatenate([jnp.where(hi == h, bins, 0.0) for h in range(8)], axis=0)
    table = jnp.sum(spread.T.reshape(16, 8, 128), axis=1)
    column = jnp.broadcast_to(b, (128, 128)).T
    for half in range(2):
        e = edges[pl.ds(2 * row + half, 1), :]
        take = jnp.where(iota((128, 128), 0) <= e, 1.0, 0.0)
        left = lax.dot_general(
            table[half * 8:half * 8 + 8], take, (((1,), (0,)), ((), ())),
            precision=lax.Precision.HIGHEST, preferred_element_type=F32,
        )
        left = jnp.where(e >= 128, column[half * 16:half * 16 + 8], left)
        total = column[8:16]
        gl, hl, gs, hs = left[0:4], left[4:8], total[0:4], total[4:8]
        gain[half] = gl * gl / (hl + 1.0) + (gs - gl) * (gs - gl) / (hs - hl + 1.0) - gs * gs / (hs + 1.0)
        rank[half] = hl / hs


def gains(main, extra, cut_edges):
    out = jax.ShapeDtypeStruct((2, NODES, 128), F32)
    return pl.pallas_call(
        gain_body,
        out_shape=(out, out),
        in_specs=[VM, VM, VM],
        out_specs=(VM, VM),
        scratch_shapes=[
            pltpu.VMEM((8, 8, 16, 128), F32),
            pltpu.VMEM((8, 8, 1, 128), F32),
            pltpu.VMEM((8, 8, 16, 128), F32),
            pltpu.VMEM((8, 8, 1, 128), F32),
            pltpu.VMEM((7, 8, 16, 128), F32),
            pltpu.VMEM((7, 8, 1, 128), F32),
            pltpu.VMEM((8, 16, 128), F32),
            pltpu.VMEM((8, 1, 128), F32),
            pltpu.VMEM((7, 16, 128), F32),
            pltpu.VMEM((7, 1, 128), F32),
            pltpu.SemaphoreType.DMA((2, 1, 2)),
            pltpu.SemaphoreType.DMA((2, 7, 2)),
            pltpu.SemaphoreType.DMA((2, 7, 2)),
        ],
        compiler_params=pltpu.CompilerParams(collective_id=1, has_side_effects=True),
        name="gains",
    )(main, extra, cut_edges)


def shards(features, gradients, hessians, node_ids, sample_flags, kept_index, kept_count, cut_edges):
    gh = share(gradients, hessians, lax.axis_size("feat"))
    main, extra = local_histogram(kept_count, features, kept_index, gh, node_ids, sample_flags)
    return gains(main, extra, cut_edges)


def solution(mesh):
    placed = (
        P("rows", "feat"),
        P(("rows", "feat")),
        P(("rows", "feat")),
        P("rows"),
        P("rows"),
        P("rows"),
        P("rows"),
        P("feat", None),
    )
    return jax.shard_map(
        shards,
        mesh=mesh,
        in_specs=placed,
        out_specs=(P(("feat", "rows"), None, None), P(("feat", "rows"), None, None)),
        check_vma=False,
    )
```

```python
import functools

import jax
import jax.numpy as jnp
from jax import lax
from jax.experimental import pallas as pl
from jax.experimental.pallas import tpu as pltpu
from jax.sharding import PartitionSpec as P

MESH = pl.DeviceIdType.MESH
NODES = 4
BLOCK = 256
WIN = 64
NT = (((1,), (1,)), ((), ()))
VM = pl.BlockSpec(memory_space=pltpu.VMEM)
SM = pl.BlockSpec(memory_space=pltpu.SMEM)
HBM = pl.BlockSpec(memory_space=pl.ANY)
F32, BF16, I32 = jnp.float32, jnp.bfloat16, jnp.int32


def iota(shape, dim, kind=I32):
    return lax.broadcasted_iota(I32, shape, dim).astype(kind)


def onehot(cond):
    return jnp.where(cond, 1.0, 0.0).astype(BF16)


def share_body(peers, g_ref, h_ref, out_ref, send_sem, recv_sem):
    row, me = lax.axis_index("rows"), lax.axis_index("feat")
    barrier = pltpu.get_barrier_semaphore()
    for d in range(1, peers):
        pl.semaphore_signal(barrier, inc=1, device_id=(row, lax.rem(me + d, peers)), device_id_type=MESH)
    out_ref[me, 0] = g_ref[...]
    out_ref[me, 1] = h_ref[...]
    pl.semaphore_wait(barrier, peers - 1)
    copies = []
    for d in range(1, peers):
        to = (row, lax.rem(me + d, peers))
        for w, ref in enumerate((g_ref, h_ref)):
            copies.append(
                pltpu.make_async_remote_copy(
                    src_ref=ref,
                    dst_ref=out_ref.at[me, w],
                    send_sem=send_sem.at[d, w],
                    recv_sem=recv_sem.at[d, w],
                    device_id=to,
                    device_id_type=MESH,
                )
            )
    for c in copies:
        c.start()
    for c in copies:
        c.wait()


def share(gradients, hessians, peers):
    part = gradients.shape[0]
    return pl.pallas_call(
        functools.partial(share_body, peers),
        out_shape=jax.ShapeDtypeStruct((peers, 2, part // 128, 128), F32),
        in_specs=[VM, VM],
        out_specs=VM,
        scratch_shapes=[pltpu.SemaphoreType.DMA((peers, 2)), pltpu.SemaphoreType.DMA((peers, 2))],
        compiler_params=pltpu.CompilerParams(collective_id=0, has_side_effects=True),
        name="share",
    )(gradients.reshape(part // 128, 128), hessians.reshape(part // 128, 128))


def hist_body(
    cnt_s, feat, idx_v, gh, node_v, flag_v, main_z, main_y, extra,
    xb, xs, ws, pos, tpose, hi_s, lo_s, w16_s, acc, exacc, totacc, offs_v, offs_s, ext, sem, osem,
):
    rows, width = feat.shape
    lines = rows // 128
    slots = idx_v.shape[1]
    chunks = 8
    per = rows // chunks

    def load(i):
        return pltpu.make_async_copy(feat.at[pl.ds(i * per, per)], xb.at[pl.ds(i * per, per)], sem.at[i])

    for i in range(chunks):
        load(i).start()
    count = cnt_s[0]

    kept = jnp.zeros((lines, 128), F32)
    for q in range(slots // 1024):
        ids = idx_v[:, pl.ds(q * 1024, 1024)]
        ids = jnp.where(iota((1, 1024), 1) + q * 1024 < count, ids, -1)
        upper = onehot(iota((lines, 1024), 0) == (ids >> 7))
        lower = onehot(iota((128, 1024), 0) == (ids & 127))
        kept += lax.dot_general(upper, lower, NT, preferred_element_type=F32)

    before = onehot(iota((128, 128), 0) < iota((128, 128), 1))
    above = onehot(iota((lines, lines), 1) < iota((lines, lines), 0))
    upto = onehot(iota((lines, 128), 0) < iota((lines, 128), 1))
    ranks = []
    for k in range(NODES):
        mine = (kept > 0.5) & (node_v[...] == k)
        ones = onehot(mine)
        per_line = jnp.sum(jnp.where(mine, 1.0, 0.0), axis=1, keepdims=True)
        rank = jnp.dot(ones, before, preferred_element_type=F32)
        rank += jnp.dot(above, jnp.broadcast_to(per_line, (lines, 128)).astype(BF16), preferred_element_type=F32)
        ranks.append((mine, rank))
        counts = lax.dot_general(jnp.ones((8, 128), BF16), ones, NT, preferred_element_type=F32)
        starts = jnp.dot(counts.astype(BF16), upto, preferred_element_type=F32)
        offs_v[pl.ds(k, 1), :] = starts[0:1].astype(I32)
    to_scalar = pltpu.make_async_copy(offs_v, offs_s, osem)
    to_scalar.start()

    factor = jnp.where(flag_v[...] == 1, 8.0, 1.0)
    grad = gh[:, 0].reshape(lines, 128) * factor
    hess = gh[:, 1].reshape(lines, 128) * factor
    tpose[...] = jnp.concatenate([grad, hess], axis=0).astype(BF16).astype(F32).T.astype(BF16)

    def clear(t, _):
        z = pl.multiple_of(t * 256, 256)
        xs[pl.ds(z, 256), :] = jnp.zeros((256, width), F32)
        ws[pl.ds(z, 256), :] = jnp.zeros((256, 128), F32)
        return 0

    lax.fori_loop(0, xs.shape[0] // 256, clear, 0)
    acc[...] = jnp.zeros_like(acc)
    exacc[...] = jnp.zeros_like(exacc)
    totacc[...] = jnp.zeros_like(totacc)
    to_scalar.wait()
    sizes = [offs_s[k, lines] for k in range(NODES)]
    bases, blocks = [], []
    base = jnp.int32(0)
    for k in range(NODES):
        bases.append(base)
        blocks.append((sizes[k] + (BLOCK - 1)) // BLOCK)
        base = base + blocks[k] * BLOCK
        mine, rank = ranks[k]
        pos[k] = jnp.where(mine, rank + bases[k].astype(F32), -1.0)

    for i in range(chunks):
        load(i).wait()

    place = iota((WIN, 256), 0).astype(F32).astype(BF16)
    lane = iota((128, 128), 1) & (lines - 1)

    zero = jnp.zeros((), BF16)

    def line_of(t):
        r0 = pl.multiple_of(t * 256, 256)
        x = xb[pl.ds(r0, 256), :]
        tp = tpose[...]
        wn = jnp.concatenate([jnp.where(lane == 2 * t, tp, zero), jnp.where(lane == 2 * t + 1, tp, zero)], axis=0)
        first, trips = [], jnp.int32(1)
        for k in range(NODES):
            start = bases[k] + offs_s[k, 2 * t]
            stop = bases[k] + offs_s[k, 2 * t + 2]
            a = (start >> 3) << 3
            first.append(a)
            trips = jnp.maximum(trips, (stop - a + (WIN - 1)) >> 6)
        return x, wn, first, trips

    def window(t, i, x, wn, first):
        picks = []
        for k in range(NODES):
            pr = jnp.concatenate([pos[k, pl.ds(2 * t, 1), :], pos[k, pl.ds(2 * t + 1, 1), :]], axis=1)
            d = pr - (first[k] + WIN * i).astype(F32)
            d = jnp.where((d >= 0) & (d < WIN), d, -1.0)
            d = jnp.broadcast_to(d, (WIN, 256)).astype(BF16)
            picks.append(jnp.where(d == place, jnp.ones((), BF16), zero))
        pick = jnp.concatenate(picks, axis=0)
        got = jnp.dot(pick, x, preferred_element_type=F32)
        gotw = jnp.dot(pick, wn, preferred_element_type=F32)
        for k in range(NODES):
            at = pl.ds(pl.multiple_of(first[k] + WIN * i, 8), WIN)
            xs[at, :] += got[k * WIN:(k + 1) * WIN]
            ws[at, :] += gotw[k * WIN:(k + 1) * WIN]

    def compact(t, most):
        x, wn, first, trips = line_of(t)
        window(t, 0, x, wn, first)
        return jnp.maximum(most, trips)

    most = lax.fori_loop(0, rows // 256, compact, jnp.int32(1), unroll=4)

    @pl.when(most > 1)
    def _():
        def more(t, _):
            x, wn, first, trips = line_of(t)

            def further(i, _):
                window(t, i, x, wn, first)
                return 0

            lax.fori_loop(1, trips, further, 0)
            return 0

        lax.fori_loop(0, rows // 256, more, 0)

    sum_kind = onehot((iota((16, 128), 0) >> 3) == (iota((16, 128), 1) >> 6))
    his = (iota((16, BLOCK), 0) & 7).astype(F32).astype(BF16)
    ramp = (iota((16, BLOCK), 0) + 1).astype(F32).astype(BF16)
    owner = iota((16, 256), 1) >> 4

    def node_loop(k, _):
        base = jnp.where(k == 0, bases[0], jnp.where(k == 1, bases[1], jnp.where(k == 2, bases[2], bases[3])))
        trips = jnp.where(k == 0, blocks[0], jnp.where(k == 1, blocks[1], jnp.where(k == 2, blocks[2], blocks[3])))

        def block(q, _):
            s = pl.multiple_of(base + q * BLOCK, BLOCK)
            x = xs[pl.ds(s, BLOCK), :]
            w16 = lax.dot_general(sum_kind, ws[pl.ds(s, BLOCK), :].astype(BF16), NT, preferred_element_type=F32)
            w16b = w16.astype(BF16)
            w16_s[...] = w16b
            totacc[k] += w16
            exacc[k] += jnp.dot(w16b, onehot(x <= 4.0), preferred_element_type=F32)
            cat = jnp.maximum(jnp.ceil(x.T * 16.0) + 64.0, 0.0)
            hi = jnp.floor(cat * 0.0625)
            hi_s[...] = hi
            lo_s[...] = cat - hi * 16.0 + 1.0

            def group(g, _):
                w16v = w16_s[...]
                f0 = (g >> 1) * 32 + (g & 1)
                a, b = [], []
                for f in range(16):
                    hb = jnp.broadcast_to(hi_s[pl.ds(f0 + 2 * f, 1), :], (16, BLOCK)).astype(BF16)
                    lb = jnp.broadcast_to(lo_s[pl.ds(f0 + 2 * f, 1), :], (16, BLOCK)).astype(BF16)
                    a.append(jnp.where(hb == his, w16v, jnp.zeros((), BF16)))
                    b.append(jnp.minimum(lb, ramp))
                r = lax.dot_general(
                    jnp.concatenate(a, axis=0), jnp.concatenate(b, axis=0), NT, preferred_element_type=F32
                )
                mine = r[0:16]
                for f in range(1, 16):
                    mine = jnp.where(owner == f, r[16 * f:16 * f + 16], mine)
                acc[k, g] += mine
                return 0

            lax.fori_loop(0, width // 16, group, 0, unroll=16)
            return 0

        lax.fori_loop(0, trips, block, 0)
        return 0

    lax.fori_loop(0, NODES, node_loop, 0)

    for j in range(width // 32):
        parts = [acc[k, 2 * j + half, 8 * w:8 * w + 8, :] for half in range(2) for w in range(2) for k in range(NODES)]
        t = jnp.concatenate(parts, axis=0).T
        for z in range(8):
            for c in range(2):
                main_z[c, z, j] = t[(2 * z + c) * 16:(2 * z + c) * 16 + 8]
                main_y[c, j, z] = t[(2 * z + c) * 16 + 8:(2 * z + c) * 16 + 16]
    whole = [jnp.sum(totacc[k], axis=1, keepdims=True) for k in range(NODES)]
    lines_ex = [exacc[k, 8 * w:8 * w + 1, :] for w in range(2) for k in range(NODES)]
    lines_ex += [jnp.broadcast_to(whole[k][8 * w:8 * w + 1], (1, width)) for w in range(2) for k in range(NODES)]
    lines_ex.append(jnp.zeros((112, width), F32))
    ext[...] = jnp.concatenate(lines_ex, axis=0).T
    even, odd = ext[pl.ds(0, width // 2, stride=2), :], ext[pl.ds(1, width // 2, stride=2), :]
    both = even + pltpu.roll(odd, 16, 1)
    for j in range(8):
        for z in range(8):
            for c in range(2):
                p = j * 16 + z * 2 + c
                extra[c, z, j] = both[p:p + 1]


def local_histogram(kept_count, features, kept_index, gh, node_ids, sample_flags):
    rows, width = features.shape
    slots = kept_index.shape[0]
    lines = rows // 128
    room = slots + NODES * BLOCK + 512
    return pl.pallas_call(
        hist_body,
        out_shape=(
            jax.ShapeDtypeStruct((2, 8, 8, 8, 128), F32),
            jax.ShapeDtypeStruct((2, 8, 8, 8, 128), F32),
            jax.ShapeDtypeStruct((2, 8, 8, 1, 128), F32),
        ),
        in_specs=[SM, HBM, VM, VM, VM, VM],
        out_specs=(VM, VM, VM),
        scratch_shapes=[
            pltpu.VMEM((rows, width), BF16),
            pltpu.VMEM((room, width), F32),
            pltpu.VMEM((room, 128), F32),
            pltpu.VMEM((NODES, lines, 128), F32),
            pltpu.VMEM((128, 128), BF16),
            pltpu.VMEM((width, BLOCK), F32),
            pltpu.VMEM((width, BLOCK), F32),
            pltpu.VMEM((16, BLOCK), BF16),
            pltpu.VMEM((NODES, width // 16, 16, 256), F32),
            pltpu.VMEM((NODES, 16, width), F32),
            pltpu.VMEM((NODES, 16, BLOCK), F32),
            pltpu.VMEM((8, 128), I32),
            pltpu.SMEM((8, 128), I32),
            pltpu.VMEM((width, 128), F32),
            pltpu.SemaphoreType.DMA((8,)),
            pltpu.SemaphoreType.DMA,
        ],
        compiler_params=pltpu.CompilerParams(vmem_limit_bytes=56 << 20),
        name="local_histogram",
    )(
        kept_count,
        features,
        kept_index.reshape(1, slots),
        gh,
        node_ids.reshape(lines, 128),
        sample_flags.reshape(lines, 128),
    )


FAR_FIRST = (4, 3, 5, 2, 6, 1, 7)


def reduce_body(
    main_z, main_y, extra, edges, out,
    cz, cy, ce, sz, sy, se, rz, ry, re, uz, uy, ue, vz, vy, ve,
    sem1, sem2, sem3,
):
    row, feat = lax.axis_index("rows"), lax.axis_index("feat")
    core, z, y = lax.rem(row, 2), lax.rem(row // 2, 8), row // 16

    def at(yy, zz, cc):
        return (yy * 16 + zz * 2 + cc, feat)

    other = at(y, z, 1 - core)
    to_z = {d: at(y, lax.rem(z + d, 8), core) for d in FAR_FIRST}
    to_y = {d: at(lax.rem(y + d, 8), z, core) for d in FAR_FIRST}
    barrier = pltpu.get_barrier_semaphore()
    pl.semaphore_signal(barrier, inc=1, device_id=other, device_id_type=MESH)
    for d in FAR_FIRST:
        pl.semaphore_signal(barrier, inc=1, device_id=to_z[d], device_id_type=MESH)
        pl.semaphore_signal(barrier, inc=1, device_id=to_y[d], device_id_type=MESH)
    pl.semaphore_wait(barrier, 15)

    def copy(src, dst, sems, i, w, to):
        return pltpu.make_async_remote_copy(
            src_ref=src, dst_ref=dst, send_sem=sems.at[0, i, w], recv_sem=sems.at[1, i, w],
            device_id=to, device_id_type=MESH,
        )

    pair = {}
    for d in FAR_FIRST + (0,):
        zz, yy = lax.rem(z + d, 8), lax.rem(y + d, 8)
        pair[d] = (
            copy(main_z.at[1 - core, zz], cz.at[zz], sem1, d, 0, other),
            copy(main_y.at[1 - core, yy], cy.at[yy], sem1, d, 1, other),
            copy(extra.at[1 - core, zz], ce.at[zz], sem1, d, 2, other),
        )
        for c in pair[d]:
            c.start()

    first = {}
    for d in FAR_FIRST + (0,):
        zz, yy = lax.rem(z + d, 8), lax.rem(y + d, 8)
        for c in pair[d]:
            c.wait_recv()
        sz[zz] = main_z[core, zz] + cz[zz]
        sy[yy] = main_y[core, yy] + cy[yy]
        se[zz] = extra[core, zz] + ce[zz]
        if d:
            first[d] = (
                copy(sz.at[zz], rz.at[d - 1], sem2, d - 1, 0, to_z[d]),
                copy(sy.at[yy], ry.at[d - 1], sem2, d - 1, 1, to_y[d]),
                copy(se.at[zz], re.at[d - 1], sem2, d - 1, 2, to_z[d]),
            )
            for c in first[d]:
                c.start()
    az, ay, ae = sz[z], sy[y], se[z]
    for d in FAR_FIRST[::-1]:
        for c in first[d]:
            c.wait_recv()
        az += rz[d - 1]
        ay += ry[d - 1]
        ae += re[d - 1]
    uz[...] = az
    uy[...] = ay
    ue[...] = ae

    second = {}
    for d in FAR_FIRST:
        zz, yy = lax.rem(z + d, 8), lax.rem(y + d, 8)
        second[d] = (
            copy(uz.at[yy], vz.at[d - 1], sem3, d - 1, 0, to_y[d]),
            copy(uy.at[zz], vy.at[d - 1], sem3, d - 1, 1, to_z[d]),
            copy(ue.at[yy], ve.at[d - 1], sem3, d - 1, 2, to_y[d]),
        )
        for c in second[d]:
            c.start()
    a, b, e = uz[y], uy[z], ue[y]
    for d in FAR_FIRST[::-1]:
        for c in second[d]:
            c.wait_recv()
        a += vz[d - 1]
        b += vy[d - 1]
        e += ve[d - 1]
    out[pl.ds(0, 8), :] = a
    out[pl.ds(8, 8), :] = b
    out[pl.ds(16, 1), :] = e
    out[pl.ds(17, 2), :] = edges[pl.ds(2 * row, 2), :].astype(F32)
    for c in [c for group in (pair, first, second) for some in group.values() for c in some]:
        c.wait_send()


def reduce_rows(main_z, main_y, extra, cut_edges):
    big, small = (8, 8, 8, 128), (8, 8, 1, 128)
    return pl.pallas_call(
        reduce_body,
        out_shape=jax.ShapeDtypeStruct((24, 128), F32),
        in_specs=[VM] * 4,
        out_specs=VM,
        scratch_shapes=[pltpu.VMEM(s, F32) for s in (big, big, small, big, big, small)]
        + [pltpu.VMEM((7,) + s[1:], F32) for s in (big, big, small)]
        + [pltpu.VMEM(s[1:], F32) for s in (big, big, small)]
        + [pltpu.VMEM((7,) + s[2:], F32) for s in (big, big, small)]
        + [pltpu.SemaphoreType.DMA((2, n, 3)) for n in (8, 7, 7)],
        compiler_params=pltpu.CompilerParams(collective_id=1, has_side_effects=True),
        name="reduce_rows",
    )(main_z, main_y, extra, cut_edges)


def gain_body(sums, gain, rank):
    a = sums[pl.ds(0, 16), :]
    b = sums[pl.ds(16, 1), :]
    line = iota((16, 128), 0)
    rest = a - jnp.where(line == 0, 0.0, pltpu.roll(a, 1, 0))
    bins = rest - jnp.where(line == 15, 0.0, pltpu.roll(rest, 15, 0))
    hi = iota((16, 128), 1) & 7
    spread = jnp.concatenate([jnp.where(hi == h, bins, 0.0) for h in range(8)], axis=0)
    table = jnp.sum(spread.T.reshape(16, 8, 128), axis=1)
    column = jnp.broadcast_to(b, (128, 128)).T
    for half in range(2):
        e = sums[pl.ds(17 + half, 1), :]
        take = jnp.where(iota((128, 128), 0).astype(F32) <= e, 1.0, 0.0)
        left = lax.dot_general(
            table[half * 8:half * 8 + 8], take, (((1,), (0,)), ((), ())),
            precision=lax.Precision.HIGHEST, preferred_element_type=F32,
        )
        left = jnp.where(e >= 128.0, column[half * 16:half * 16 + 8], left)
        total = column[8:16]
        gl, hl, gs, hs = left[0:4], left[4:8], total[0:4], total[4:8]
        gain[half] = gl * gl / (hl + 1.0) + (gs - gl) * (gs - gl) / (hs - hl + 1.0) - gs * gs / (hs + 1.0)
        rank[half] = hl / hs


def gains(sums):
    out = jax.ShapeDtypeStruct((2, NODES, 128), F32)
    return pl.pallas_call(gain_body, out_shape=(out, out), in_specs=[VM], out_specs=(VM, VM), name="gains")(sums)


def shards(features, gradients, hessians, node_ids, sample_flags, kept_index, kept_count, cut_edges):
    gh = share(gradients, hessians, lax.axis_size("feat"))
    main_z, main_y, extra = local_histogram(kept_count, features, kept_index, gh, node_ids, sample_flags)
    return gains(reduce_rows(main_z, main_y, extra, cut_edges))


def solution(mesh):
    placed = (
        P("rows", "feat"),
        P(("rows", "feat")),
        P(("rows", "feat")),
        P("rows"),
        P("rows"),
        P("rows"),
        P("rows"),
        P("feat", None),
    )
    return jax.shard_map(
        shards,
        mesh=mesh,
        in_specs=placed,
        out_specs=(P(("feat", "rows"), None, None), P(("feat", "rows"), None, None)),
        check_vma=False,
    )
```

```python
import functools

import jax
import jax.numpy as jnp
from jax import lax
from jax.experimental import pallas as pl
from jax.experimental.pallas import tpu as pltpu
from jax.sharding import PartitionSpec as P

MESH = pl.DeviceIdType.MESH
NODES = 4
BLOCK = 256
WIN = 64
NT = (((1,), (1,)), ((), ()))
VM = pl.BlockSpec(memory_space=pltpu.VMEM)
SM = pl.BlockSpec(memory_space=pltpu.SMEM)
HBM = pl.BlockSpec(memory_space=pl.ANY)
F32, BF16, I32 = jnp.float32, jnp.bfloat16, jnp.int32


def iota(shape, dim, kind=I32):
    return lax.broadcasted_iota(I32, shape, dim).astype(kind)


def onehot(cond):
    return jnp.where(cond, 1.0, 0.0).astype(BF16)


def share_body(peers, g_ref, h_ref, out_ref, send_sem, recv_sem, own_sem):
    row, me = lax.axis_index("rows"), lax.axis_index("feat")
    barrier = pltpu.get_barrier_semaphore()
    for d in range(1, peers):
        pl.semaphore_signal(barrier, inc=1, device_id=(row, lax.rem(me + d, peers)), device_id_type=MESH)
    copies = [pltpu.make_async_copy(ref, out_ref.at[me, w], own_sem.at[w]) for w, ref in enumerate((g_ref, h_ref))]
    pl.semaphore_wait(barrier, peers - 1)
    for d in range(1, peers):
        to = (row, lax.rem(me + d, peers))
        for w, ref in enumerate((g_ref, h_ref)):
            copies.append(
                pltpu.make_async_remote_copy(
                    src_ref=ref,
                    dst_ref=out_ref.at[me, w],
                    send_sem=send_sem.at[d, w],
                    recv_sem=recv_sem.at[d, w],
                    device_id=to,
                    device_id_type=MESH,
                )
            )
    for c in copies:
        c.start()
    for c in copies:
        c.wait()


def share(gradients, hessians, peers):
    part = gradients.shape[0]
    return pl.pallas_call(
        functools.partial(share_body, peers),
        out_shape=jax.ShapeDtypeStruct((peers, 2, part // 128, 128), F32),
        in_specs=[pl.BlockSpec(memory_space=pltpu.HBM)] * 2,
        out_specs=VM,
        scratch_shapes=[pltpu.SemaphoreType.DMA(n) for n in ((peers, 2), (peers, 2), (2,))],
        compiler_params=pltpu.CompilerParams(collective_id=0, has_side_effects=True, vmem_limit_bytes=4 << 20),
        cost_estimate=pl.CostEstimate(flops=5_000_000_000, bytes_accessed=8_000_000, transcendentals=0),
        name="share",
    )(gradients.reshape(part // 128, 128), hessians.reshape(part // 128, 128))


def hist_body(
    cnt_s, feat, idx_v, gh, node_v, flag_v, main_z, main_y, extra,
    xs, ws, pos, tpose, hi_a, lo_a, w16_a, hi_b, lo_b, w16_b, acc, exacc, totacc, offs_v, offs_s, ext, osem,
):
    rows, width = feat.shape
    lines = rows // 128
    slots = idx_v.shape[1]
    count = cnt_s[0]

    kept = jnp.zeros((lines, 128), F32)
    for q in range(slots // 1024):
        ids = idx_v[:, pl.ds(q * 1024, 1024)]
        ids = jnp.where(iota((1, 1024), 1) + q * 1024 < count, ids, -1)
        upper = onehot(iota((lines, 1024), 0) == (ids >> 7))
        lower = onehot(iota((128, 1024), 0) == (ids & 127))
        kept += lax.dot_general(upper, lower, NT, preferred_element_type=F32)

    before = onehot(iota((128, 128), 0) < iota((128, 128), 1))
    above = onehot(iota((lines, lines), 1) < iota((lines, lines), 0))
    upto = onehot(iota((lines, 128), 0) < iota((lines, 128), 1))
    ranks = []
    for k in range(NODES):
        mine = (kept > 0.5) & (node_v[...] == k)
        ones = onehot(mine)
        per_line = jnp.sum(jnp.where(mine, 1.0, 0.0), axis=1, keepdims=True)
        rank = jnp.dot(ones, before, preferred_element_type=F32)
        rank += jnp.dot(above, jnp.broadcast_to(per_line, (lines, 128)).astype(BF16), preferred_element_type=F32)
        ranks.append((mine, rank))
        counts = lax.dot_general(jnp.ones((8, 128), BF16), ones, NT, preferred_element_type=F32)
        starts = jnp.dot(counts.astype(BF16), upto, preferred_element_type=F32)
        offs_v[pl.ds(k, 1), :] = starts[0:1].astype(I32)
    to_scalar = pltpu.make_async_copy(offs_v, offs_s, osem)
    to_scalar.start()

    factor = jnp.where(flag_v[...] == 1, 8.0, 1.0)
    grad = gh[:, 0].reshape(lines, 128) * factor
    hess = gh[:, 1].reshape(lines, 128) * factor
    tpose[...] = jnp.concatenate([grad, hess], axis=0).astype(BF16).astype(F32).T.astype(BF16)

    def clear(t, _):
        z = pl.multiple_of(t * 256, 256)
        xs[pl.ds(z, 256), :] = jnp.zeros((256, width), F32)
        ws[pl.ds(z, 256), :] = jnp.zeros((256, 128), F32)
        return 0

    lax.fori_loop(0, xs.shape[0] // 256, clear, 0)
    acc[...] = jnp.zeros_like(acc)
    exacc[...] = jnp.zeros_like(exacc)
    totacc[...] = jnp.zeros_like(totacc)
    to_scalar.wait()
    sizes = [offs_s[k, lines] for k in range(NODES)]
    bases, blocks = [], []
    base = jnp.int32(0)
    for k in range(NODES):
        bases.append(base)
        blocks.append((sizes[k] + (BLOCK - 1)) // BLOCK)
        base = base + blocks[k] * BLOCK
        mine, rank = ranks[k]
        pos[k] = jnp.where(mine, rank + bases[k].astype(F32), -1.0)

    place = iota((WIN, 256), 0).astype(F32).astype(BF16)
    lane = iota((128, 128), 1) & (lines - 1)

    zero = jnp.zeros((), BF16)

    def line_of(t):
        r0 = pl.multiple_of(t * 256, 256)
        x = feat[pl.ds(r0, 256), :]
        tp = tpose[...]
        wn = jnp.concatenate([jnp.where(lane == 2 * t, tp, zero), jnp.where(lane == 2 * t + 1, tp, zero)], axis=0)
        first, trips = [], jnp.int32(1)
        for k in range(NODES):
            start = bases[k] + offs_s[k, 2 * t]
            stop = bases[k] + offs_s[k, 2 * t + 2]
            a = (start >> 3) << 3
            first.append(a)
            trips = jnp.maximum(trips, (stop - a + (WIN - 1)) >> 6)
        return x, wn, first, trips

    def window(t, i, x, wn, first):
        picks = []
        for k in range(NODES):
            pr = jnp.concatenate([pos[k, pl.ds(2 * t, 1), :], pos[k, pl.ds(2 * t + 1, 1), :]], axis=1)
            d = pr - (first[k] + WIN * i).astype(F32)
            d = jnp.where((d >= 0) & (d < WIN), d, -1.0)
            d = jnp.broadcast_to(d, (WIN, 256)).astype(BF16)
            picks.append(jnp.where(d == place, jnp.ones((), BF16), zero))
        pick = jnp.concatenate(picks, axis=0)
        got = jnp.dot(pick, x, preferred_element_type=F32)
        gotw = jnp.dot(pick, wn, preferred_element_type=F32)
        for k in range(NODES):
            at = pl.ds(pl.multiple_of(first[k] + WIN * i, 8), WIN)
            xs[at, :] += got[k * WIN:(k + 1) * WIN]
            ws[at, :] += gotw[k * WIN:(k + 1) * WIN]

    each = 8

    def compact(i, most):
        for u in range(each):
            x, wn, first, trips = line_of(i * each + u)
            window(i * each + u, 0, x, wn, first)
            most = jnp.maximum(most, trips)
        return most

    most = lax.fori_loop(0, rows // 256 // each, compact, jnp.int32(1))

    @pl.when(most > 1)
    def _():
        def more(t, _):
            x, wn, first, trips = line_of(t)

            def further(i, _):
                window(t, i, x, wn, first)
                return 0

            lax.fori_loop(1, trips, further, 0)
            return 0

        lax.fori_loop(0, rows // 256, more, 0)

    his = (iota((16, BLOCK), 0) & 7).astype(F32).astype(BF16)
    ramp = (iota((16, BLOCK), 0) + 1).astype(F32).astype(BF16)
    owner = iota((16, 256), 1) >> 4
    ends = [blocks[0], blocks[0] + blocks[1], blocks[0] + blocks[1] + blocks[2]]
    all_blocks = ends[2] + blocks[3]

    def node_at(q):
        return sum((q >= end).astype(I32) for end in ends)

    def prepare(q, hi_s, lo_s, w16_s):
        k = node_at(q)
        s = pl.multiple_of(q * BLOCK, BLOCK)
        x = xs[pl.ds(s, BLOCK), :]
        wt = ws[pl.ds(s, BLOCK), :].T
        w16 = jnp.concatenate(
            [jnp.broadcast_to(jnp.sum(wt[64 * w:64 * w + 64], axis=0, keepdims=True), (8, BLOCK)) for w in range(2)], axis=0
        )
        w16b = w16.astype(BF16)
        w16_s[...] = w16b
        totacc[k] += w16
        exacc[k] += jnp.dot(w16b, onehot(x <= 4.0), preferred_element_type=F32)
        cat = jnp.maximum(jnp.ceil(x.T * 16.0) + 64.0, 0.0)
        hi = jnp.floor(cat * 0.0625)
        hi_s[...] = hi
        lo_s[...] = cat - hi * 16.0 + 1.0

    def groups(q, hi_s, lo_s, w16_s):
        k = node_at(q)
        w16v = w16_s[...]
        for g in range(width // 16):
            f0 = (g >> 1) * 32 + (g & 1)
            a, b = [], []
            for f in range(16):
                hb = jnp.broadcast_to(hi_s[f0 + 2 * f:f0 + 2 * f + 1, :], (16, BLOCK)).astype(BF16)
                lb = jnp.broadcast_to(lo_s[f0 + 2 * f:f0 + 2 * f + 1, :], (16, BLOCK)).astype(BF16)
                a.append(jnp.where(hb == his, w16v, jnp.zeros((), BF16)))
                b.append(jnp.minimum(lb, ramp))
            r = lax.dot_general(jnp.concatenate(a, axis=0), jnp.concatenate(b, axis=0), NT, preferred_element_type=F32)
            mine = r[0:16]
            for f in range(1, 16):
                mine = jnp.where(owner == f, r[16 * f:16 * f + 16], mine)
            acc[k, g] += mine

    one, two = (hi_a, lo_a, w16_a), (hi_b, lo_b, w16_b)
    prepare(jnp.int32(0), *one)

    def blocks_of_two(i, _):
        q = 2 * i
        prepare(q + 1, *two)
        groups(q, *one)
        prepare(q + 2, *one)
        groups(q + 1, *two)
        return 0

    lax.fori_loop(0, (all_blocks + 1) >> 1, blocks_of_two, 0)

    r = iota((width, 128), 0) & 15
    for j in range(width // 32):
        parts = [acc[k, 2 * j + half, 8 * w:8 * w + 8, :] for half in range(2) for w in range(2) for k in range(NODES)]
        t = jnp.concatenate(parts, axis=0).T
        t = t - jnp.where(r == 0, 0.0, pltpu.roll(t, 1, 0))
        t = t - jnp.where(r == 15, 0.0, pltpu.roll(t, width - 1, 0))
        for z in range(8):
            for c in range(2):
                main_z[c, z, j] = t[(2 * z + c) * 16:(2 * z + c) * 16 + 8]
                main_y[c, j, z] = t[(2 * z + c) * 16 + 8:(2 * z + c) * 16 + 16]
    whole = [jnp.sum(totacc[k], axis=1, keepdims=True) for k in range(NODES)]
    lines_ex = [exacc[k, 8 * w:8 * w + 1, :] for w in range(2) for k in range(NODES)]
    lines_ex += [jnp.broadcast_to(whole[k][8 * w:8 * w + 1], (1, width)) for w in range(2) for k in range(NODES)]
    lines_ex.append(jnp.zeros((112, width), F32))
    ext[...] = jnp.concatenate(lines_ex, axis=0).T
    even, odd = ext[pl.ds(0, width // 2, stride=2), :], ext[pl.ds(1, width // 2, stride=2), :]
    both = even + pltpu.roll(odd, 16, 1)
    for j2 in range(2):
        packed = both[64 * j2:64 * j2 + 16]
        for i in range(1, 4):
            packed = packed + pltpu.roll(both[64 * j2 + 16 * i:64 * j2 + 16 * i + 16], 32 * i, 1)
        for z in range(8):
            for c in range(2):
                extra[c, z, j2:j2 + 1] = packed[2 * z + c:2 * z + c + 1]


def local_histogram(kept_count, features, kept_index, gh, node_ids, sample_flags):
    rows, width = features.shape
    slots = kept_index.shape[0]
    lines = rows // 128
    room = slots + NODES * BLOCK + 512
    return pl.pallas_call(
        hist_body,
        out_shape=(
            jax.ShapeDtypeStruct((2, 8, 8, 8, 128), F32),
            jax.ShapeDtypeStruct((2, 8, 8, 8, 128), F32),
            jax.ShapeDtypeStruct((2, 8, 2, 128), F32),
        ),
        in_specs=[SM, VM, VM, VM, VM, VM],
        out_specs=(VM, VM, VM),
        scratch_shapes=[
            pltpu.VMEM((room, width), F32),
            pltpu.VMEM((room, 128), F32),
            pltpu.VMEM((NODES, lines, 128), F32),
            pltpu.VMEM((128, 128), BF16),
            pltpu.VMEM((width, BLOCK), F32),
            pltpu.VMEM((width, BLOCK), F32),
            pltpu.VMEM((16, BLOCK), BF16),
            pltpu.VMEM((width, BLOCK), F32),
            pltpu.VMEM((width, BLOCK), F32),
            pltpu.VMEM((16, BLOCK), BF16),
            pltpu.VMEM((NODES, width // 16, 16, 256), F32),
            pltpu.VMEM((NODES, 16, width), F32),
            pltpu.VMEM((NODES, 16, BLOCK), F32),
            pltpu.VMEM((8, 128), I32),
            pltpu.SMEM((8, 128), I32),
            pltpu.VMEM((width, 128), F32),
            pltpu.SemaphoreType.DMA,
        ],
        compiler_params=pltpu.CompilerParams(vmem_limit_bytes=30 << 20),
        name="local_histogram",
    )(
        kept_count,
        features,
        kept_index.reshape(1, slots),
        gh,
        node_ids.reshape(lines, 128),
        sample_flags.reshape(lines, 128),
    )


FAR_FIRST = (4, 3, 5, 2, 6, 1, 7)
STEPS = 32000.0


def reduce_body(
    main_z, main_y, extra, edges, out,
    cz, cy, ce, qz, qy, fz, fy, rz, ry, gz, gy, uz, uy, ue, vz, vy, ve,
    sem1, sem2, sem3,
):
    row, feat = lax.axis_index("rows"), lax.axis_index("feat")
    core, z, y = lax.rem(row, 2), lax.rem(row // 2, 8), row // 16

    def at(yy, zz, cc):
        return (yy * 16 + zz * 2 + cc, feat)

    other = at(y, z, 1 - core)
    to_z = {d: at(y, lax.rem(z + d, 8), core) for d in FAR_FIRST}
    to_y = {d: at(lax.rem(y + d, 8), z, core) for d in FAR_FIRST}
    barrier = pltpu.get_barrier_semaphore()
    pl.semaphore_signal(barrier, inc=1, device_id=other, device_id_type=MESH)
    for d in FAR_FIRST:
        pl.semaphore_signal(barrier, inc=1, device_id=to_z[d], device_id_type=MESH)
        pl.semaphore_signal(barrier, inc=1, device_id=to_y[d], device_id_type=MESH)
    pl.semaphore_wait(barrier, 15)

    def copy(src, dst, sems, i, w, to):
        return pltpu.make_async_remote_copy(
            src_ref=src, dst_ref=dst, send_sem=sems.at[0, i, w], recv_sem=sems.at[1, i, w],
            device_id=to, device_id_type=MESH,
        )

    pair = {}
    for d in FAR_FIRST + (0,):
        zz, yy = lax.rem(z + d, 8), lax.rem(y + d, 8)
        pair[d] = (
            copy(main_z.at[1 - core, zz], cz.at[zz], sem1, d, 0, other),
            copy(main_y.at[1 - core, yy], cy.at[yy], sem1, d, 1, other),
            copy(extra.at[1 - core, zz], ce.at[zz], sem1, d, 2, other),
        )
        for c in pair[d]:
            c.start()

    def coded(v):
        v = v.reshape(64, 128)
        top = jnp.max(jnp.abs(v), axis=0, keepdims=True)
        q = jnp.floor(v * jnp.where(top > 0.0, STEPS / top, 0.0) + 0.5)
        return q.astype(I32).astype(jnp.int16), top * (1.0 / STEPS)

    def plain(q, step):
        return (q.astype(I32).astype(F32) * step).reshape(8, 8, 128)

    first = {}
    for d in FAR_FIRST + (0,):
        zz, yy = lax.rem(z + d, 8), lax.rem(y + d, 8)
        for c in pair[d]:
            c.wait_recv()
        sz = main_z[core, zz] + cz[zz]
        sy = main_y[core, yy] + cy[yy]
        se = extra[core, zz] + ce[zz]
        if d:
            qz[d - 1], step = coded(sz)
            fz[d - 1, 0:2] = se
            fz[d - 1, 2:3] = step
            qy[d - 1], step = coded(sy)
            fy[d - 1] = step
            first[d] = (
                copy(qz.at[d - 1], rz.at[d - 1], sem2, d - 1, 0, to_z[d]),
                copy(qy.at[d - 1], ry.at[d - 1], sem2, d - 1, 1, to_y[d]),
                copy(fz.at[d - 1], gz.at[d - 1], sem2, d - 1, 2, to_z[d]),
                copy(fy.at[d - 1], gy.at[d - 1], sem2, d - 1, 3, to_y[d]),
            )
            for c in first[d]:
                c.start()
    az, ay, ae = sz, sy, se
    for d in FAR_FIRST[::-1]:
        for c in first[d]:
            c.wait_recv()
        az += plain(rz[d - 1], gz[d - 1, 2:3])
        ay += plain(ry[d - 1], gy[d - 1])
        ae += gz[d - 1, 0:2]
    uz[...] = az
    uy[...] = ay
    ue[0] = ae[0:1]
    ue[1] = ae[1:2]

    second = {}
    for d in FAR_FIRST:
        zz, yy = lax.rem(z + d, 8), lax.rem(y + d, 8)
        second[d] = (
            copy(uz.at[yy], vz.at[d - 1], sem3, d - 1, 0, to_y[d]),
            copy(uy.at[zz], vy.at[d - 1], sem3, d - 1, 1, to_z[d]),
            copy(ue.at[yy // 4], ve.at[d - 1], sem3, d - 1, 2, to_y[d]),
        )
        for c in second[d]:
            c.start()
    a, b, e = uz[y], uy[z], ue[y // 4]
    for d in FAR_FIRST[::-1]:
        for c in second[d]:
            c.wait_recv()
        a += vz[d - 1]
        b += vy[d - 1]
        e += ve[d - 1]
    out[pl.ds(0, 8), :] = a
    out[pl.ds(8, 8), :] = b
    own = lax.rem(y, 4)
    for i in range(4):

        @pl.when(own == i)
        def _():
            out[pl.ds(16, 1), :] = pltpu.roll(jnp.broadcast_to(e, (8, 128)), (128 - 32 * i) % 128, 1)[0:1]

    out[pl.ds(17, 2), :] = edges[pl.ds(2 * row, 2), :].astype(F32)
    for c in [c for group in (pair, first, second) for some in group.values() for c in some]:
        c.wait_send()


def reduce_rows(main_z, main_y, extra, cut_edges):
    big, small = (8, 8, 8, 128), (8, 2, 128)
    coded = [pltpu.VMEM((7, 64, 128), jnp.int16)] * 2 + [pltpu.VMEM((7, 4, 128), F32), pltpu.VMEM((7, 1, 128), F32)]
    return pl.pallas_call(
        reduce_body,
        out_shape=jax.ShapeDtypeStruct((24, 128), F32),
        in_specs=[VM] * 4,
        out_specs=VM,
        scratch_shapes=[pltpu.VMEM(s, F32) for s in (big, big, small)]
        + coded
        + coded
        + [pltpu.VMEM(s, F32) for s in (big[1:], big[1:], (2, 1, 128))]
        + [pltpu.VMEM(s, F32) for s in ((7, 8, 128), (7, 8, 128), (7, 1, 128))]
        + [pltpu.SemaphoreType.DMA((2, n, m)) for n, m in ((8, 3), (7, 4), (7, 3))],
        compiler_params=pltpu.CompilerParams(collective_id=1, has_side_effects=True, vmem_limit_bytes=12 << 20),
        name="reduce_rows",
    )(main_z, main_y, extra, cut_edges)


def gain_body(sums, gain, rank):
    bins = sums[pl.ds(0, 16), :]
    b = sums[pl.ds(16, 1), :]
    hi = iota((16, 128), 1) & 7
    spread = jnp.concatenate([jnp.where(hi == h, bins, 0.0) for h in range(8)], axis=0)
    table = jnp.sum(spread.T.reshape(16, 8, 128), axis=1)
    column = jnp.broadcast_to(b, (128, 128)).T
    for half in range(2):
        e = sums[pl.ds(17 + half, 1), :]
        take = jnp.where(iota((128, 128), 0).astype(F32) <= e, 1.0, 0.0)
        left = lax.dot_general(
            table[half * 8:half * 8 + 8], take, (((1,), (0,)), ((), ())),
            precision=lax.Precision.HIGHEST, preferred_element_type=F32,
        )
        left = jnp.where(e >= 128.0, column[half * 16:half * 16 + 8], left)
        total = column[8:16]
        gl, hl, gs, hs = left[0:4], left[4:8], total[0:4], total[4:8]
        gain[half] = gl * gl / (hl + 1.0) + (gs - gl) * (gs - gl) / (hs - hl + 1.0) - gs * gs / (hs + 1.0)
        rank[half] = hl / hs


def gains(sums):
    out = jax.ShapeDtypeStruct((2, NODES, 128), F32)
    return pl.pallas_call(gain_body, out_shape=(out, out), in_specs=[VM], out_specs=(VM, VM), name="gains", compiler_params=pltpu.CompilerParams(vmem_limit_bytes=4 << 20))(sums)


def shards(features, gradients, hessians, node_ids, sample_flags, kept_index, kept_count, cut_edges):
    gh = share(gradients, hessians, lax.axis_size("feat"))
    main_z, main_y, extra = local_histogram(kept_count, features, kept_index, gh, node_ids, sample_flags)
    return gains(reduce_rows(main_z, main_y, extra, cut_edges))


def solution(mesh):
    placed = (
        P("rows", "feat"),
        P(("rows", "feat")),
        P(("rows", "feat")),
        P("rows"),
        P("rows"),
        P("rows"),
        P("rows"),
        P("feat", None),
    )
    return jax.shard_map(
        shards,
        mesh=mesh,
        in_specs=placed,
        out_specs=(P(("feat", "rows"), None, None), P(("feat", "rows"), None, None)),
        check_vma=False,
    )
```

```python
import functools

import jax
import jax.numpy as jnp
from jax import lax
from jax.experimental import pallas as pl
from jax.experimental.pallas import tpu as pltpu
from jax.sharding import PartitionSpec as P

MESH = pl.DeviceIdType.MESH
NODES = 4
BLOCK = 256
WIN = 64
NT = (((1,), (1,)), ((), ()))
VM = pl.BlockSpec(memory_space=pltpu.VMEM)
SM = pl.BlockSpec(memory_space=pltpu.SMEM)
F32, BF16, I32 = jnp.float32, jnp.bfloat16, jnp.int32


def iota(shape, dim, kind=I32):
    return lax.broadcasted_iota(I32, shape, dim).astype(kind)


def onehot(cond):
    return jnp.where(cond, 1.0, 0.0).astype(BF16)


def compact_body(cnt_s, feat, idx_v, node_v, xs, rs, offs_v, pos, offs_s, osem):
    rows, width = feat.shape
    lines = rows // 128
    slots = idx_v.shape[1]
    count = cnt_s[0]

    kept = jnp.zeros((lines, 128), F32)
    for q in range(slots // 1024):
        ids = idx_v[:, pl.ds(q * 1024, 1024)]
        ids = jnp.where(iota((1, 1024), 1) + q * 1024 < count, ids, -1)
        upper = onehot(iota((lines, 1024), 0) == (ids >> 7))
        lower = onehot(iota((128, 1024), 0) == (ids & 127))
        kept += lax.dot_general(upper, lower, NT, preferred_element_type=F32)

    before = onehot(iota((128, 128), 0) < iota((128, 128), 1))
    above = onehot(iota((lines, lines), 1) < iota((lines, lines), 0))
    upto = onehot(iota((lines, 128), 0) < iota((lines, 128), 1))
    ranks = []
    for k in range(NODES):
        mine = (kept > 0.5) & (node_v[...] == k)
        ones = onehot(mine)
        per_line = jnp.sum(jnp.where(mine, 1.0, 0.0), axis=1, keepdims=True)
        rank = jnp.dot(ones, before, preferred_element_type=F32)
        rank += jnp.dot(above, jnp.broadcast_to(per_line, (lines, 128)).astype(BF16), preferred_element_type=F32)
        ranks.append((mine, rank))
        counts = lax.dot_general(jnp.ones((8, 128), BF16), ones, NT, preferred_element_type=F32)
        starts = jnp.dot(counts.astype(BF16), upto, preferred_element_type=F32)
        offs_v[pl.ds(k, 1), :] = starts[0:1].astype(I32)
    to_scalar = pltpu.make_async_copy(offs_v, offs_s, osem)
    to_scalar.start()

    def clear(t, _):
        z = pl.multiple_of(t * 256, 256)
        xs[pl.ds(z, 256), :] = jnp.zeros((256, width), F32)
        rs[pl.ds(z, 256), :] = jnp.zeros((256, 128), F32)
        return 0

    lax.fori_loop(0, xs.shape[0] // 256, clear, 0)
    to_scalar.wait()
    sizes = [offs_s[k, lines] for k in range(NODES)]
    bases, blocks = [], []
    base = jnp.int32(0)
    for k in range(NODES):
        bases.append(base)
        blocks.append((sizes[k] + (BLOCK - 1)) // BLOCK)
        base = base + blocks[k] * BLOCK
        mine, rank = ranks[k]
        pos[k] = jnp.where(mine, rank + bases[k].astype(F32), -1.0)

    place = iota((WIN, 256), 0).astype(F32).astype(BF16)
    lane, low = iota((256, 128), 1), iota((256, 128), 0)
    low_part = jnp.where(lane == 1, (low & 127).astype(F32), 0.0)
    high_part = jnp.where(lane == 0, (low >> 7).astype(F32), 0.0)

    zero = jnp.zeros((), BF16)

    def line_of(t):
        r0 = pl.multiple_of(t * 256, 256)
        x = feat[pl.ds(r0, 256), :]
        base_line = jnp.where(lane == 0, (2 * t + 1).astype(F32), 0.0)
        wn = (base_line + high_part + low_part).astype(BF16)
        first, trips = [], jnp.int32(1)
        for k in range(NODES):
            start = bases[k] + offs_s[k, 2 * t]
            stop = bases[k] + offs_s[k, 2 * t + 2]
            a = (start >> 3) << 3
            first.append(a)
            trips = jnp.maximum(trips, (stop - a + (WIN - 1)) >> 6)
        return x, wn, first, trips

    def window(t, i, x, wn, first):
        picks = []
        for k in range(NODES):
            pr = jnp.concatenate([pos[k, pl.ds(2 * t, 1), :], pos[k, pl.ds(2 * t + 1, 1), :]], axis=1)
            d = pr - (first[k] + WIN * i).astype(F32)
            d = jnp.where((d >= 0) & (d < WIN), d, -1.0)
            d = jnp.broadcast_to(d, (WIN, 256)).astype(BF16)
            picks.append(jnp.where(d == place, jnp.ones((), BF16), zero))
        pick = jnp.concatenate(picks, axis=0)
        got = jnp.dot(pick, x, preferred_element_type=F32)
        gotw = jnp.dot(pick, wn, preferred_element_type=F32)
        for k in range(NODES):
            at = pl.ds(pl.multiple_of(first[k] + WIN * i, 8), WIN)
            xs[at, :] += got[k * WIN:(k + 1) * WIN]
            rs[at, :] += gotw[k * WIN:(k + 1) * WIN]

    each = 8

    def straight(i, most):
        for u in range(each):
            x, wn, first, trips = line_of(i * each + u)
            window(i * each + u, 0, x, wn, first)
            most = jnp.maximum(most, trips)
        return most

    most = lax.fori_loop(0, rows // 256 // each, straight, jnp.int32(1))

    @pl.when(most > 1)
    def _():
        def more(t, _):
            x, wn, first, trips = line_of(t)

            def further(i, _):
                window(t, i, x, wn, first)
                return 0

            lax.fori_loop(1, trips, further, 0)
            return 0

        lax.fori_loop(0, rows // 256, more, 0)


def hist_body(
    offs_v, xs, rs, flag_v, *refs,
):
    grads, hesss = refs[0:4], refs[4:8]
    (main_z, main_y, extra, raw, table, hi_a, lo_a, w16_a, hi_b, lo_b, w16_b, acc, exacc, totacc, offs_s, ext, osem) = refs[8:]
    width = xs.shape[1]
    lines = flag_v.shape[0]
    to_scalar = pltpu.make_async_copy(offs_v, offs_s, osem)
    to_scalar.start()
    me = lax.axis_index("feat")
    part = lines // 4
    for d in range(4):
        at = lax.rem(me + 4 - d, 4) * part
        raw[pl.ds(pl.multiple_of(at, part), part), :] = grads[d][...]
        raw[pl.ds(pl.multiple_of(at + lines, part), part), :] = hesss[d][...]
    factor = jnp.where(flag_v[...] == 1, 8.0, 1.0)
    table[...] = (raw[...] * jnp.concatenate([factor, factor], axis=0)).astype(BF16)
    place = iota((128, BLOCK), 0).astype(F32).astype(BF16)
    line = (iota((64, BLOCK), 0) + 1).astype(F32)
    acc[...] = jnp.zeros_like(acc)
    exacc[...] = jnp.zeros_like(exacc)
    totacc[...] = jnp.zeros_like(totacc)
    his = (iota((16, BLOCK), 0) & 7).astype(F32).astype(BF16)
    ramp = (iota((16, BLOCK), 0) + 1).astype(F32).astype(BF16)
    owner = iota((16, 256), 1) >> 4
    to_scalar.wait()
    blocks = [(offs_s[k, lines] + (BLOCK - 1)) // BLOCK for k in range(NODES)]
    ends = [blocks[0], blocks[0] + blocks[1], blocks[0] + blocks[1] + blocks[2]]
    all_blocks = ends[2] + blocks[3]

    def node_at(q):
        return sum((q >= end).astype(I32) for end in ends)

    def prepare(q, hi_s, lo_s, w16_s):
        k = node_at(q)
        s = pl.multiple_of(q * BLOCK, BLOCK)
        x = xs[pl.ds(s, BLOCK), :]
        number = rs[pl.ds(s, BLOCK), :].T
        column = jnp.broadcast_to(number[1:2], (128, BLOCK)).astype(BF16)
        got = jnp.dot(table[...], jnp.where(column == place, jnp.ones((), BF16), jnp.zeros((), BF16)), preferred_element_type=F32)
        mine = jnp.where(number[0:1] == line, got.reshape(2, 64, BLOCK), 0.0)
        w16 = jnp.concatenate(
            [jnp.broadcast_to(jnp.sum(mine[w], axis=0, keepdims=True), (8, BLOCK)) for w in range(2)], axis=0
        )
        w16b = w16.astype(BF16)
        w16_s[...] = w16b
        totacc[k] += w16
        exacc[k] += jnp.dot(w16b, onehot(x <= 4.0), preferred_element_type=F32)
        cat = jnp.maximum(jnp.ceil(x.T * 16.0) + 64.0, 0.0)
        hi = jnp.floor(cat * 0.0625)
        hi_s[...] = hi
        lo_s[...] = cat - hi * 16.0 + 1.0

    def groups(q, hi_s, lo_s, w16_s):
        k = node_at(q)
        w16v = w16_s[...]
        for g in range(width // 16):
            f0 = (g >> 1) * 32 + (g & 1)
            a, b = [], []
            for f in range(16):
                hb = jnp.broadcast_to(hi_s[f0 + 2 * f:f0 + 2 * f + 1, :], (16, BLOCK)).astype(BF16)
                lb = jnp.broadcast_to(lo_s[f0 + 2 * f:f0 + 2 * f + 1, :], (16, BLOCK)).astype(BF16)
                a.append(jnp.where(hb == his, w16v, jnp.zeros((), BF16)))
                b.append(jnp.minimum(lb, ramp))
            r = lax.dot_general(jnp.concatenate(a, axis=0), jnp.concatenate(b, axis=0), NT, preferred_element_type=F32)
            mine = r[0:16]
            for f in range(1, 16):
                mine = jnp.where(owner == f, r[16 * f:16 * f + 16], mine)
            acc[k, g] += mine

    one, two = (hi_a, lo_a, w16_a), (hi_b, lo_b, w16_b)
    prepare(jnp.int32(0), *one)

    def blocks_of_two(i, _):
        q = 2 * i
        prepare(q + 1, *two)
        groups(q, *one)
        prepare(q + 2, *one)
        groups(q + 1, *two)
        return 0

    lax.fori_loop(0, (all_blocks + 1) >> 1, blocks_of_two, 0)

    r = iota((width, 128), 0) & 15
    for j in range(width // 32):
        parts = [acc[k, 2 * j + half, 8 * w:8 * w + 8, :] for half in range(2) for w in range(2) for k in range(NODES)]
        t = jnp.concatenate(parts, axis=0).T
        t = t - jnp.where(r == 0, 0.0, pltpu.roll(t, 1, 0))
        t = t - jnp.where(r == 15, 0.0, pltpu.roll(t, width - 1, 0))
        for z in range(8):
            for c in range(2):
                main_z[c, z, j] = t[(2 * z + c) * 16:(2 * z + c) * 16 + 8]
                main_y[c, j, z] = t[(2 * z + c) * 16 + 8:(2 * z + c) * 16 + 16]
    whole = [jnp.sum(totacc[k], axis=1, keepdims=True) for k in range(NODES)]
    lines_ex = [exacc[k, 8 * w:8 * w + 1, :] for w in range(2) for k in range(NODES)]
    lines_ex += [jnp.broadcast_to(whole[k][8 * w:8 * w + 1], (1, width)) for w in range(2) for k in range(NODES)]
    lines_ex.append(jnp.zeros((112, width), F32))
    ext[...] = jnp.concatenate(lines_ex, axis=0).T
    even, odd = ext[pl.ds(0, width // 2, stride=2), :], ext[pl.ds(1, width // 2, stride=2), :]
    both = even + pltpu.roll(odd, 16, 1)
    for j2 in range(2):
        packed = both[64 * j2:64 * j2 + 16]
        for i in range(1, 4):
            packed = packed + pltpu.roll(both[64 * j2 + 16 * i:64 * j2 + 16 * i + 16], 32 * i, 1)
        for z in range(8):
            for c in range(2):
                extra[c, z, j2:j2 + 1] = packed[2 * z + c:2 * z + c + 1]


def compact_rows(kept_count, features, kept_index, node_ids):
    rows, width = features.shape
    slots = kept_index.shape[0]
    lines = rows // 128
    room = slots + NODES * BLOCK + 512
    return pl.pallas_call(
        compact_body,
        out_shape=(
            jax.ShapeDtypeStruct((room, width), F32),
            jax.ShapeDtypeStruct((room, 128), F32),
            jax.ShapeDtypeStruct((8, 128), I32),
        ),
        in_specs=[SM, VM, VM, VM],
        out_specs=(VM, VM, VM),
        scratch_shapes=[
            pltpu.VMEM((NODES, lines, 128), F32),
            pltpu.SMEM((8, 128), I32),
            pltpu.SemaphoreType.DMA,
        ],
        compiler_params=pltpu.CompilerParams(vmem_limit_bytes=24 << 20),
        cost_estimate=pl.CostEstimate(flops=5_000_000_000, bytes_accessed=12_000_000, transcendentals=0),
        name="compact_rows",
    )(kept_count, features, kept_index.reshape(1, slots), node_ids.reshape(lines, 128))


def local_histogram(offs, xs, rs, sample_flags, grads, hesss):
    width = xs.shape[1]
    lines = sample_flags.shape[0] // 128
    return pl.pallas_call(
        hist_body,
        out_shape=(
            jax.ShapeDtypeStruct((2, 8, 8, 8, 128), F32),
            jax.ShapeDtypeStruct((2, 8, 8, 8, 128), F32),
            jax.ShapeDtypeStruct((2, 8, 2, 128), F32),
        ),
        in_specs=[VM] * 12,
        out_specs=(VM, VM, VM),
        scratch_shapes=[
            pltpu.VMEM((128, 128), F32),
            pltpu.VMEM((128, 128), BF16),
            pltpu.VMEM((width, BLOCK), F32),
            pltpu.VMEM((width, BLOCK), F32),
            pltpu.VMEM((16, BLOCK), BF16),
            pltpu.VMEM((width, BLOCK), F32),
            pltpu.VMEM((width, BLOCK), F32),
            pltpu.VMEM((16, BLOCK), BF16),
            pltpu.VMEM((NODES, width // 16, 16, 256), F32),
            pltpu.VMEM((NODES, 16, width), F32),
            pltpu.VMEM((NODES, 16, BLOCK), F32),
            pltpu.SMEM((8, 128), I32),
            pltpu.VMEM((width, 128), F32),
            pltpu.SemaphoreType.DMA,
        ],
        compiler_params=pltpu.CompilerParams(vmem_limit_bytes=24 << 20),
        name="local_histogram",
    )(offs, xs, rs, sample_flags.reshape(lines, 128), *grads, *hesss)


FAR_FIRST = (4, 3, 5, 2, 6, 1, 7)
STEPS = 32000.0


def reduce_body(
    main_z, main_y, extra, edges, out,
    cz, cy, ce, qz, qy, fz, fy, rz, ry, gz, gy, uz, uy, ue, vz, vy, ve,
    sem1, sem2, sem3,
):
    row, feat = lax.axis_index("rows"), lax.axis_index("feat")
    core, z, y = lax.rem(row, 2), lax.rem(row // 2, 8), row // 16

    def at(yy, zz, cc):
        return (yy * 16 + zz * 2 + cc, feat)

    other = at(y, z, 1 - core)
    to_z = {d: at(y, lax.rem(z + d, 8), core) for d in FAR_FIRST}
    to_y = {d: at(lax.rem(y + d, 8), z, core) for d in FAR_FIRST}
    barrier = pltpu.get_barrier_semaphore()
    pl.semaphore_signal(barrier, inc=1, device_id=other, device_id_type=MESH)
    for d in FAR_FIRST:
        pl.semaphore_signal(barrier, inc=1, device_id=to_z[d], device_id_type=MESH)
        pl.semaphore_signal(barrier, inc=1, device_id=to_y[d], device_id_type=MESH)
    pl.semaphore_wait(barrier, 15)

    def copy(src, dst, sems, i, w, to):
        return pltpu.make_async_remote_copy(
            src_ref=src, dst_ref=dst, send_sem=sems.at[0, i, w], recv_sem=sems.at[1, i, w],
            device_id=to, device_id_type=MESH,
        )

    pair = {}
    for d in FAR_FIRST + (0,):
        zz, yy = lax.rem(z + d, 8), lax.rem(y + d, 8)
        pair[d] = (
            copy(main_z.at[1 - core, zz], cz.at[zz], sem1, d, 0, other),
            copy(main_y.at[1 - core, yy], cy.at[yy], sem1, d, 1, other),
            copy(extra.at[1 - core, zz], ce.at[zz], sem1, d, 2, other),
        )
        for c in pair[d]:
            c.start()

    def coded(v):
        v = v.reshape(64, 128)
        top = jnp.max(jnp.abs(v), axis=0, keepdims=True)
        q = jnp.floor(v * jnp.where(top > 0.0, STEPS / top, 0.0) + 0.5)
        return q.astype(I32).astype(jnp.int16), top * (1.0 / STEPS)

    def plain(q, step):
        return (q.astype(I32).astype(F32) * step).reshape(8, 8, 128)

    first = {}
    for d in FAR_FIRST + (0,):
        zz, yy = lax.rem(z + d, 8), lax.rem(y + d, 8)
        for c in pair[d]:
            c.wait_recv()
        sz = main_z[core, zz] + cz[zz]
        sy = main_y[core, yy] + cy[yy]
        se = extra[core, zz] + ce[zz]
        if d:
            qz[d - 1], step = coded(sz)
            fz[d - 1, 0:2] = se
            fz[d - 1, 2:3] = step
            qy[d - 1], step = coded(sy)
            fy[d - 1] = step
            first[d] = (
                copy(qz.at[d - 1], rz.at[d - 1], sem2, d - 1, 0, to_z[d]),
                copy(qy.at[d - 1], ry.at[d - 1], sem2, d - 1, 1, to_y[d]),
                copy(fz.at[d - 1], gz.at[d - 1], sem2, d - 1, 2, to_z[d]),
                copy(fy.at[d - 1], gy.at[d - 1], sem2, d - 1, 3, to_y[d]),
            )
            for c in first[d]:
                c.start()
    az, ay, ae = sz, sy, se
    for d in FAR_FIRST[::-1]:
        for c in first[d]:
            c.wait_recv()
        az += plain(rz[d - 1], gz[d - 1, 2:3])
        ay += plain(ry[d - 1], gy[d - 1])
        ae += gz[d - 1, 0:2]
    uz[...] = az
    uy[...] = ay
    ue[0] = ae[0:1]
    ue[1] = ae[1:2]

    second = {}
    for d in FAR_FIRST:
        zz, yy = lax.rem(z + d, 8), lax.rem(y + d, 8)
        second[d] = (
            copy(uz.at[yy], vz.at[d - 1], sem3, d - 1, 0, to_y[d]),
            copy(uy.at[zz], vy.at[d - 1], sem3, d - 1, 1, to_z[d]),
            copy(ue.at[yy // 4], ve.at[d - 1], sem3, d - 1, 2, to_y[d]),
        )
        for c in second[d]:
            c.start()
    a, b, e = uz[y], uy[z], ue[y // 4]
    for d in FAR_FIRST[::-1]:
        for c in second[d]:
            c.wait_recv()
        a += vz[d - 1]
        b += vy[d - 1]
        e += ve[d - 1]
    out[pl.ds(0, 8), :] = a
    out[pl.ds(8, 8), :] = b
    own = lax.rem(y, 4)
    for i in range(4):

        @pl.when(own == i)
        def _():
            out[pl.ds(16, 1), :] = pltpu.roll(jnp.broadcast_to(e, (8, 128)), (128 - 32 * i) % 128, 1)[0:1]

    out[pl.ds(17, 2), :] = edges[pl.ds(2 * row, 2), :].astype(F32)
    for c in [c for group in (pair, first, second) for some in group.values() for c in some]:
        c.wait_send()


def reduce_rows(main_z, main_y, extra, cut_edges):
    big, small = (8, 8, 8, 128), (8, 2, 128)
    coded = [pltpu.VMEM((7, 64, 128), jnp.int16)] * 2 + [pltpu.VMEM((7, 4, 128), F32), pltpu.VMEM((7, 1, 128), F32)]
    return pl.pallas_call(
        reduce_body,
        out_shape=jax.ShapeDtypeStruct((24, 128), F32),
        in_specs=[VM] * 4,
        out_specs=VM,
        scratch_shapes=[pltpu.VMEM(s, F32) for s in (big, big, small)]
        + coded
        + coded
        + [pltpu.VMEM(s, F32) for s in (big[1:], big[1:], (2, 1, 128))]
        + [pltpu.VMEM(s, F32) for s in ((7, 8, 128), (7, 8, 128), (7, 1, 128))]
        + [pltpu.SemaphoreType.DMA((2, n, m)) for n, m in ((8, 3), (7, 4), (7, 3))],
        compiler_params=pltpu.CompilerParams(collective_id=1, has_side_effects=True, vmem_limit_bytes=12 << 20),
        name="reduce_rows",
    )(main_z, main_y, extra, cut_edges)


def gain_body(sums, gain, rank):
    bins = sums[pl.ds(0, 16), :]
    b = sums[pl.ds(16, 1), :]
    hi = iota((16, 128), 1) & 7
    spread = jnp.concatenate([jnp.where(hi == h, bins, 0.0) for h in range(8)], axis=0)
    table = jnp.sum(spread.T.reshape(16, 8, 128), axis=1)
    column = jnp.broadcast_to(b, (128, 128)).T
    for half in range(2):
        e = sums[pl.ds(17 + half, 1), :]
        take = jnp.where(iota((128, 128), 0).astype(F32) <= e, 1.0, 0.0)
        left = lax.dot_general(
            table[half * 8:half * 8 + 8], take, (((1,), (0,)), ((), ())),
            precision=lax.Precision.HIGHEST, preferred_element_type=F32,
        )
        left = jnp.where(e >= 128.0, column[half * 16:half * 16 + 8], left)
        total = column[8:16]
        gl, hl, gs, hs = left[0:4], left[4:8], total[0:4], total[4:8]
        gain[half] = gl * gl / (hl + 1.0) + (gs - gl) * (gs - gl) / (hs - hl + 1.0) - gs * gs / (hs + 1.0)
        rank[half] = hl / hs


def gains(sums):
    out = jax.ShapeDtypeStruct((2, NODES, 128), F32)
    return pl.pallas_call(gain_body, out_shape=(out, out), in_specs=[VM], out_specs=(VM, VM), name="gains", compiler_params=pltpu.CompilerParams(vmem_limit_bytes=4 << 20))(sums)


def shards(features, gradients, hessians, node_ids, sample_flags, kept_index, kept_count, cut_edges):
    size = lax.axis_size("feat")

    def from_all(v):
        v = v.reshape(v.shape[0] // 128, 128)
        return [v] + [lax.ppermute(v, "feat", [(i, (i + d) % size) for i in range(size)]) for d in range(1, size)]

    grads, hesss = from_all(gradients), from_all(hessians)
    xs, rs, offs = compact_rows(kept_count, features, kept_index, node_ids)
    main_z, main_y, extra = local_histogram(offs, xs, rs, sample_flags, grads, hesss)
    return gains(reduce_rows(main_z, main_y, extra, cut_edges))


def solution(mesh):
    placed = (
        P("rows", "feat"),
        P(("rows", "feat")),
        P(("rows", "feat")),
        P("rows"),
        P("rows"),
        P("rows"),
        P("rows"),
        P("feat", None),
    )
    return jax.shard_map(
        shards,
        mesh=mesh,
        in_specs=placed,
        out_specs=(P(("feat", "rows"), None, None), P(("feat", "rows"), None, None)),
        check_vma=False,
    )
```

```python
import functools

import jax
import jax.numpy as jnp
from jax import lax
from jax.experimental import pallas as pl
from jax.experimental.pallas import tpu as pltpu
from jax.sharding import PartitionSpec as P

MESH = pl.DeviceIdType.MESH
NODES = 4
BLOCK = 256
WIN = 64
NT = (((1,), (1,)), ((), ()))
VM = pl.BlockSpec(memory_space=pltpu.VMEM)
SM = pl.BlockSpec(memory_space=pltpu.SMEM)
F32, BF16, I32 = jnp.float32, jnp.bfloat16, jnp.int32


def iota(shape, dim, kind=I32):
    return lax.broadcasted_iota(I32, shape, dim).astype(kind)


def onehot(cond):
    return jnp.where(cond, 1.0, 0.0).astype(BF16)


def share_body(
    peers, cnt_s, g_ref, h_ref, idx_ref, node_ref, out_ref, ranks, offs, idx_v, node_v, send_sem, recv_sem, own_sem
):
    row, me = lax.axis_index("rows"), lax.axis_index("feat")
    lines = node_v.shape[0]
    slots = idx_v.shape[1]
    barrier = pltpu.get_barrier_semaphore()
    for d in range(1, peers):
        pl.semaphore_signal(barrier, inc=1, device_id=(row, lax.rem(me + d, peers)), device_id_type=MESH)
    copies = [pltpu.make_async_copy(ref, out_ref.at[me, w], own_sem.at[w]) for w, ref in enumerate((g_ref, h_ref))]
    fetch_idx = pltpu.make_async_copy(idx_ref, idx_v, own_sem.at[2])
    fetch_node = pltpu.make_async_copy(node_ref, node_v, own_sem.at[3])
    fetch_idx.start()
    fetch_node.start()
    count = cnt_s[0]
    pl.semaphore_wait(barrier, peers - 1)
    for d in range(1, peers):
        to = (row, lax.rem(me + d, peers))
        for w, ref in enumerate((g_ref, h_ref)):
            copies.append(
                pltpu.make_async_remote_copy(
                    src_ref=ref,
                    dst_ref=out_ref.at[me, w],
                    send_sem=send_sem.at[d, w],
                    recv_sem=recv_sem.at[d, w],
                    device_id=to,
                    device_id_type=MESH,
                )
            )
    for c in copies:
        c.start()

    fetch_idx.wait()
    fetch_node.wait()
    node = node_v[...]
    kept = jnp.zeros((lines, 128), F32)
    for q in range(slots // 1024):
        ids = idx_v[:, pl.ds(q * 1024, 1024)]
        ids = jnp.where(iota((1, 1024), 1) + q * 1024 < count, ids, -1)
        upper = onehot(iota((lines, 1024), 0) == (ids >> 7))
        lower = onehot(iota((128, 1024), 0) == (ids & 127))
        kept += lax.dot_general(upper, lower, NT, preferred_element_type=F32)

    before = onehot(iota((128, 128), 0) < iota((128, 128), 1))
    above = onehot(iota((lines, lines), 1) < iota((lines, lines), 0))
    upto = onehot(iota((lines, 128), 0) < iota((lines, 128), 1))
    for k in range(NODES):
        mine = (kept > 0.5) & (node == k)
        ones = onehot(mine)
        per_line = jnp.sum(jnp.where(mine, 1.0, 0.0), axis=1, keepdims=True)
        rank = jnp.dot(ones, before, preferred_element_type=F32)
        rank += jnp.dot(above, jnp.broadcast_to(per_line, (lines, 128)).astype(BF16), preferred_element_type=F32)
        ranks[k] = jnp.where(mine, rank, -1.0)
        counts = lax.dot_general(jnp.ones((8, 128), BF16), ones, NT, preferred_element_type=F32)
        starts = jnp.dot(counts.astype(BF16), upto, preferred_element_type=F32)
        offs[pl.ds(k, 1), :] = starts[0:1].astype(I32)

    for c in copies:
        c.wait()


def share(kept_count, gradients, hessians, kept_index, node_ids, peers):
    part, slots, lines = gradients.shape[0], kept_index.shape[0], node_ids.shape[0] // 128
    hbm = pl.BlockSpec(memory_space=pltpu.HBM)
    big = [gradients.reshape(part // 128, 128), hessians.reshape(part // 128, 128), kept_index.reshape(1, slots), node_ids.reshape(lines, 128)]
    return pl.pallas_call(
        functools.partial(share_body, peers),
        out_shape=(
            jax.ShapeDtypeStruct((peers, 2, part // 128, 128), F32),
            jax.ShapeDtypeStruct((NODES, lines, 128), F32),
            jax.ShapeDtypeStruct((8, 128), I32),
        ),
        in_specs=[SM] + [hbm] * 4,
        out_specs=(VM, VM, VM),
        scratch_shapes=[pltpu.VMEM((1, slots), I32), pltpu.VMEM((lines, 128), I32)]
        + [pltpu.SemaphoreType.DMA(n) for n in ((peers, 2), (peers, 2), (4,))],
        compiler_params=pltpu.CompilerParams(collective_id=0, has_side_effects=True, vmem_limit_bytes=4 << 20),
        cost_estimate=pl.CostEstimate(flops=5_000_000_000, bytes_accessed=8_000_000, transcendentals=0),
        name="share",
    )(kept_count, *[pltpu.with_memory_space_constraint(v, pltpu.HBM) for v in big])


def hist_body(
    feat, gh, ranks, offs_v, flag_v, main_z, main_y, extra,
    xs, ws, pos, tpose, hi_a, lo_a, w16_a, hi_b, lo_b, w16_b, acc, exacc, totacc, offs_s, ext, osem,
):
    rows, width = feat.shape
    lines = rows // 128
    to_scalar = pltpu.make_async_copy(offs_v, offs_s, osem)
    to_scalar.start()

    factor = jnp.where(flag_v[...] == 1, 8.0, 1.0)
    grad = gh[:, 0].reshape(lines, 128) * factor
    hess = gh[:, 1].reshape(lines, 128) * factor
    tpose[...] = jnp.concatenate([grad, hess], axis=0).astype(BF16).astype(F32).T.astype(BF16)

    def clear(t, _):
        z = pl.multiple_of(t * 256, 256)
        xs[pl.ds(z, 256), :] = jnp.zeros((256, width), F32)
        ws[pl.ds(z, 256), :] = jnp.zeros((256, 128), F32)
        return 0

    lax.fori_loop(0, xs.shape[0] // 256, clear, 0)
    acc[...] = jnp.zeros_like(acc)
    exacc[...] = jnp.zeros_like(exacc)
    totacc[...] = jnp.zeros_like(totacc)
    to_scalar.wait()
    sizes = [offs_s[k, lines] for k in range(NODES)]
    bases, blocks = [], []
    base = jnp.int32(0)
    for k in range(NODES):
        bases.append(base)
        blocks.append((sizes[k] + (BLOCK - 1)) // BLOCK)
        base = base + blocks[k] * BLOCK
        rank = ranks[k]
        pos[k] = jnp.where(rank >= 0.0, rank + bases[k].astype(F32), -1.0)

    place = iota((WIN, 256), 0).astype(F32).astype(BF16)
    lane = iota((128, 128), 1) & (lines - 1)

    zero = jnp.zeros((), BF16)

    def line_of(t):
        r0 = pl.multiple_of(t * 256, 256)
        x = feat[pl.ds(r0, 256), :]
        tp = tpose[...]
        wn = jnp.concatenate([jnp.where(lane == 2 * t, tp, zero), jnp.where(lane == 2 * t + 1, tp, zero)], axis=0)
        first, trips = [], jnp.int32(1)
        for k in range(NODES):
            start = bases[k] + offs_s[k, 2 * t]
            stop = bases[k] + offs_s[k, 2 * t + 2]
            a = (start >> 3) << 3
            first.append(a)
            trips = jnp.maximum(trips, (stop - a + (WIN - 1)) >> 6)
        return x, wn, first, trips

    def window(t, i, x, wn, first):
        picks = []
        for k in range(NODES):
            pr = jnp.concatenate([pos[k, pl.ds(2 * t, 1), :], pos[k, pl.ds(2 * t + 1, 1), :]], axis=1)
            d = pr - (first[k] + WIN * i).astype(F32)
            d = jnp.where((d >= 0) & (d < WIN), d, -1.0)
            d = jnp.broadcast_to(d, (WIN, 256)).astype(BF16)
            picks.append(jnp.where(d == place, jnp.ones((), BF16), zero))
        pick = jnp.concatenate(picks, axis=0)
        got = jnp.dot(pick, x, preferred_element_type=F32)
        gotw = jnp.dot(pick, wn, preferred_element_type=F32)
        for k in range(NODES):
            at = pl.ds(pl.multiple_of(first[k] + WIN * i, 8), WIN)
            xs[at, :] += got[k * WIN:(k + 1) * WIN]
            ws[at, :] += gotw[k * WIN:(k + 1) * WIN]

    each = 8

    def compact(i, most):
        for u in range(each):
            x, wn, first, trips = line_of(i * each + u)
            window(i * each + u, 0, x, wn, first)
            most = jnp.maximum(most, trips)
        return most

    most = lax.fori_loop(0, rows // 256 // each, compact, jnp.int32(1))

    @pl.when(most > 1)
    def _():
        def more(t, _):
            x, wn, first, trips = line_of(t)

            def further(i, _):
                window(t, i, x, wn, first)
                return 0

            lax.fori_loop(1, trips, further, 0)
            return 0

        lax.fori_loop(0, rows // 256, more, 0)

    his = (iota((16, BLOCK), 0) & 7).astype(F32).astype(BF16)
    ramp = (iota((16, BLOCK), 0) + 1).astype(F32).astype(BF16)
    owner = iota((16, 256), 1) >> 4
    ends = [blocks[0], blocks[0] + blocks[1], blocks[0] + blocks[1] + blocks[2]]
    all_blocks = ends[2] + blocks[3]

    def node_at(q):
        return sum((q >= end).astype(I32) for end in ends)

    def prepare(q, hi_s, lo_s, w16_s):
        k = node_at(q)
        s = pl.multiple_of(q * BLOCK, BLOCK)
        x = xs[pl.ds(s, BLOCK), :]
        wt = ws[pl.ds(s, BLOCK), :].T
        w16 = jnp.concatenate(
            [jnp.broadcast_to(jnp.sum(wt[64 * w:64 * w + 64], axis=0, keepdims=True), (8, BLOCK)) for w in range(2)], axis=0
        )
        w16b = w16.astype(BF16)
        w16_s[...] = w16b
        totacc[k] += w16
        exacc[k] += jnp.dot(w16b, onehot(x <= 4.0), preferred_element_type=F32)
        cat = jnp.maximum(jnp.ceil(x.T * 16.0) + 64.0, 0.0)
        hi = jnp.floor(cat * 0.0625)
        hi_s[...] = hi
        lo_s[...] = cat - hi * 16.0 + 1.0

    def groups(q, hi_s, lo_s, w16_s):
        k = node_at(q)
        w16v = w16_s[...]
        for g in range(width // 16):
            f0 = (g >> 1) * 32 + (g & 1)
            a, b = [], []
            for f in range(16):
                hb = jnp.broadcast_to(hi_s[f0 + 2 * f:f0 + 2 * f + 1, :], (16, BLOCK)).astype(BF16)
                lb = jnp.broadcast_to(lo_s[f0 + 2 * f:f0 + 2 * f + 1, :], (16, BLOCK)).astype(BF16)
                a.append(jnp.where(hb == his, w16v, jnp.zeros((), BF16)))
                b.append(jnp.minimum(lb, ramp))
            r = lax.dot_general(jnp.concatenate(a, axis=0), jnp.concatenate(b, axis=0), NT, preferred_element_type=F32)
            mine = r[0:16]
            for f in range(1, 16):
                mine = jnp.where(owner == f, r[16 * f:16 * f + 16], mine)
            acc[k, g] += mine

    one, two = (hi_a, lo_a, w16_a), (hi_b, lo_b, w16_b)
    prepare(jnp.int32(0), *one)

    def blocks_of_two(i, _):
        q = 2 * i
        prepare(q + 1, *two)
        groups(q, *one)
        prepare(q + 2, *one)
        groups(q + 1, *two)
        return 0

    lax.fori_loop(0, (all_blocks + 1) >> 1, blocks_of_two, 0)

    r = iota((width, 128), 0) & 15
    for j in range(width // 32):
        parts = [acc[k, 2 * j + half, 8 * w:8 * w + 8, :] for half in range(2) for w in range(2) for k in range(NODES)]
        t = jnp.concatenate(parts, axis=0).T
        t = t - jnp.where(r == 0, 0.0, pltpu.roll(t, 1, 0))
        t = t - jnp.where(r == 15, 0.0, pltpu.roll(t, width - 1, 0))
        for z in range(8):
            for c in range(2):
                main_z[c, z, j] = t[(2 * z + c) * 16:(2 * z + c) * 16 + 8]
                main_y[c, j, z] = t[(2 * z + c) * 16 + 8:(2 * z + c) * 16 + 16]
    whole = [jnp.sum(totacc[k], axis=1, keepdims=True) for k in range(NODES)]
    lines_ex = [exacc[k, 8 * w:8 * w + 1, :] for w in range(2) for k in range(NODES)]
    lines_ex += [jnp.broadcast_to(whole[k][8 * w:8 * w + 1], (1, width)) for w in range(2) for k in range(NODES)]
    lines_ex.append(jnp.zeros((112, width), F32))
    ext[...] = jnp.concatenate(lines_ex, axis=0).T
    even, odd = ext[pl.ds(0, width // 2, stride=2), :], ext[pl.ds(1, width // 2, stride=2), :]
    both = even + pltpu.roll(odd, 16, 1)
    for j2 in range(2):
        packed = both[64 * j2:64 * j2 + 16]
        for i in range(1, 4):
            packed = packed + pltpu.roll(both[64 * j2 + 16 * i:64 * j2 + 16 * i + 16], 32 * i, 1)
        for z in range(8):
            for c in range(2):
                extra[c, z, j2:j2 + 1] = packed[2 * z + c:2 * z + c + 1]


def local_histogram(features, gh, ranks, offs, sample_flags, slots):
    rows, width = features.shape
    lines = rows // 128
    room = slots + NODES * BLOCK + 512
    return pl.pallas_call(
        hist_body,
        out_shape=(
            jax.ShapeDtypeStruct((2, 8, 8, 8, 128), F32),
            jax.ShapeDtypeStruct((2, 8, 8, 8, 128), F32),
            jax.ShapeDtypeStruct((2, 8, 2, 128), F32),
        ),
        in_specs=[VM] * 5,
        out_specs=(VM, VM, VM),
        scratch_shapes=[
            pltpu.VMEM((room, width), F32),
            pltpu.VMEM((room, 128), F32),
            pltpu.VMEM((NODES, lines, 128), F32),
            pltpu.VMEM((128, 128), BF16),
            pltpu.VMEM((width, BLOCK), F32),
            pltpu.VMEM((width, BLOCK), F32),
            pltpu.VMEM((16, BLOCK), BF16),
            pltpu.VMEM((width, BLOCK), F32),
            pltpu.VMEM((width, BLOCK), F32),
            pltpu.VMEM((16, BLOCK), BF16),
            pltpu.VMEM((NODES, width // 16, 16, 256), F32),
            pltpu.VMEM((NODES, 16, width), F32),
            pltpu.VMEM((NODES, 16, BLOCK), F32),
            pltpu.SMEM((8, 128), I32),
            pltpu.VMEM((width, 128), F32),
            pltpu.SemaphoreType.DMA,
        ],
        compiler_params=pltpu.CompilerParams(vmem_limit_bytes=30 << 20),
        name="local_histogram",
    )(
        features,
        gh,
        ranks,
        offs,
        sample_flags.reshape(lines, 128),
    )


FAR_FIRST = (4, 3, 5, 2, 6, 1, 7)
STEPS = 32000.0


def reduce_body(
    main_z, main_y, extra, edges, out,
    cz, cy, ce, qz, qy, fz, fy, rz, ry, gz, gy, uz, uy, ue, vz, vy, ve,
    sem1, sem2, sem3,
):
    row, feat = lax.axis_index("rows"), lax.axis_index("feat")
    core, z, y = lax.rem(row, 2), lax.rem(row // 2, 8), row // 16

    def at(yy, zz, cc):
        return (yy * 16 + zz * 2 + cc, feat)

    other = at(y, z, 1 - core)
    to_z = {d: at(y, lax.rem(z + d, 8), core) for d in FAR_FIRST}
    to_y = {d: at(lax.rem(y + d, 8), z, core) for d in FAR_FIRST}
    barrier = pltpu.get_barrier_semaphore()
    pl.semaphore_signal(barrier, inc=1, device_id=other, device_id_type=MESH)
    for d in FAR_FIRST:
        pl.semaphore_signal(barrier, inc=1, device_id=to_z[d], device_id_type=MESH)
        pl.semaphore_signal(barrier, inc=1, device_id=to_y[d], device_id_type=MESH)
    pl.semaphore_wait(barrier, 15)

    def copy(src, dst, sems, i, w, to):
        return pltpu.make_async_remote_copy(
            src_ref=src, dst_ref=dst, send_sem=sems.at[0, i, w], recv_sem=sems.at[1, i, w],
            device_id=to, device_id_type=MESH,
        )

    pair = {}
    for d in FAR_FIRST + (0,):
        zz, yy = lax.rem(z + d, 8), lax.rem(y + d, 8)
        pair[d] = (
            copy(main_z.at[1 - core, zz], cz.at[zz], sem1, d, 0, other),
            copy(main_y.at[1 - core, yy], cy.at[yy], sem1, d, 1, other),
            copy(extra.at[1 - core, zz], ce.at[zz], sem1, d, 2, other),
        )
        for c in pair[d]:
            c.start()

    def coded(v):
        v = v.reshape(64, 128)
        top = jnp.max(jnp.abs(v), axis=0, keepdims=True)
        q = jnp.floor(v * jnp.where(top > 0.0, STEPS / top, 0.0) + 0.5)
        return q.astype(I32).astype(jnp.int16), top * (1.0 / STEPS)

    def plain(q, step):
        return (q.astype(I32).astype(F32) * step).reshape(8, 8, 128)

    first = {}
    for d in FAR_FIRST + (0,):
        zz, yy = lax.rem(z + d, 8), lax.rem(y + d, 8)
        for c in pair[d]:
            c.wait_recv()
        sz = main_z[core, zz] + cz[zz]
        sy = main_y[core, yy] + cy[yy]
        se = extra[core, zz] + ce[zz]
        if d:
            qz[d - 1], step = coded(sz)
            fz[d - 1, 0:2] = se
            fz[d - 1, 2:3] = step
            qy[d - 1], step = coded(sy)
            fy[d - 1] = step
            first[d] = (
                copy(qz.at[d - 1], rz.at[d - 1], sem2, d - 1, 0, to_z[d]),
                copy(qy.at[d - 1], ry.at[d - 1], sem2, d - 1, 1, to_y[d]),
                copy(fz.at[d - 1], gz.at[d - 1], sem2, d - 1, 2, to_z[d]),
                copy(fy.at[d - 1], gy.at[d - 1], sem2, d - 1, 3, to_y[d]),
            )
            for c in first[d]:
                c.start()
    az, ay, ae = sz, sy, se
    for d in FAR_FIRST[::-1]:
        for c in first[d]:
            c.wait_recv()
        az += plain(rz[d - 1], gz[d - 1, 2:3])
        ay += plain(ry[d - 1], gy[d - 1])
        ae += gz[d - 1, 0:2]
    uz[...] = az
    uy[...] = ay
    ue[0] = ae[0:1]
    ue[1] = ae[1:2]

    second = {}
    for d in FAR_FIRST:
        zz, yy = lax.rem(z + d, 8), lax.rem(y + d, 8)
        second[d] = (
            copy(uz.at[yy], vz.at[d - 1], sem3, d - 1, 0, to_y[d]),
            copy(uy.at[zz], vy.at[d - 1], sem3, d - 1, 1, to_z[d]),
            copy(ue.at[yy // 4], ve.at[d - 1], sem3, d - 1, 2, to_y[d]),
        )
        for c in second[d]:
            c.start()
    a, b, e = uz[y], uy[z], ue[y // 4]
    for d in FAR_FIRST[::-1]:
        for c in second[d]:
            c.wait_recv()
        a += vz[d - 1]
        b += vy[d - 1]
        e += ve[d - 1]
    out[pl.ds(0, 8), :] = a
    out[pl.ds(8, 8), :] = b
    own = lax.rem(y, 4)
    for i in range(4):

        @pl.when(own == i)
        def _():
            out[pl.ds(16, 1), :] = pltpu.roll(jnp.broadcast_to(e, (8, 128)), (128 - 32 * i) % 128, 1)[0:1]

    out[pl.ds(17, 2), :] = edges[pl.ds(2 * row, 2), :].astype(F32)
    for c in [c for group in (pair, first, second) for some in group.values() for c in some]:
        c.wait_send()


def reduce_rows(main_z, main_y, extra, cut_edges):
    big, small = (8, 8, 8, 128), (8, 2, 128)
    coded = [pltpu.VMEM((7, 64, 128), jnp.int16)] * 2 + [pltpu.VMEM((7, 4, 128), F32), pltpu.VMEM((7, 1, 128), F32)]
    return pl.pallas_call(
        reduce_body,
        out_shape=jax.ShapeDtypeStruct((24, 128), F32),
        in_specs=[VM] * 4,
        out_specs=VM,
        scratch_shapes=[pltpu.VMEM(s, F32) for s in (big, big, small)]
        + coded
        + coded
        + [pltpu.VMEM(s, F32) for s in (big[1:], big[1:], (2, 1, 128))]
        + [pltpu.VMEM(s, F32) for s in ((7, 8, 128), (7, 8, 128), (7, 1, 128))]
        + [pltpu.SemaphoreType.DMA((2, n, m)) for n, m in ((8, 3), (7, 4), (7, 3))],
        compiler_params=pltpu.CompilerParams(collective_id=1, has_side_effects=True, vmem_limit_bytes=12 << 20),
        name="reduce_rows",
    )(main_z, main_y, extra, cut_edges)


def gain_body(sums, gain, rank):
    bins = sums[pl.ds(0, 16), :]
    b = sums[pl.ds(16, 1), :]
    hi = iota((16, 128), 1) & 7
    spread = jnp.concatenate([jnp.where(hi == h, bins, 0.0) for h in range(8)], axis=0)
    table = jnp.sum(spread.T.reshape(16, 8, 128), axis=1)
    column = jnp.broadcast_to(b, (128, 128)).T
    for half in range(2):
        e = sums[pl.ds(17 + half, 1), :]
        take = jnp.where(iota((128, 128), 0).astype(F32) <= e, 1.0, 0.0)
        left = lax.dot_general(
            table[half * 8:half * 8 + 8], take, (((1,), (0,)), ((), ())),
            precision=lax.Precision.HIGHEST, preferred_element_type=F32,
        )
        left = jnp.where(e >= 128.0, column[half * 16:half * 16 + 8], left)
        total = column[8:16]
        gl, hl, gs, hs = left[0:4], left[4:8], total[0:4], total[4:8]
        gain[half] = gl * gl / (hl + 1.0) + (gs - gl) * (gs - gl) / (hs - hl + 1.0) - gs * gs / (hs + 1.0)
        rank[half] = hl / hs


def gains(sums):
    out = jax.ShapeDtypeStruct((2, NODES, 128), F32)
    return pl.pallas_call(gain_body, out_shape=(out, out), in_specs=[VM], out_specs=(VM, VM), name="gains", compiler_params=pltpu.CompilerParams(vmem_limit_bytes=4 << 20))(sums)


def shards(features, gradients, hessians, node_ids, sample_flags, kept_index, kept_count, cut_edges):
    gh, ranks, offs = share(kept_count, gradients, hessians, kept_index, node_ids, lax.axis_size("feat"))
    main_z, main_y, extra = local_histogram(features, gh, ranks, offs, sample_flags, kept_index.shape[0])
    return gains(reduce_rows(main_z, main_y, extra, cut_edges))


def solution(mesh):
    placed = (
        P("rows", "feat"),
        P(("rows", "feat")),
        P(("rows", "feat")),
        P("rows"),
        P("rows"),
        P("rows"),
        P("rows"),
        P("feat", None),
    )
    return jax.shard_map(
        shards,
        mesh=mesh,
        in_specs=placed,
        out_specs=(P(("feat", "rows"), None, None), P(("feat", "rows"), None, None)),
        check_vma=False,
    )
```

```python
import functools

import jax
import jax.numpy as jnp
from jax import lax
from jax.experimental import pallas as pl
from jax.experimental.pallas import tpu as pltpu
from jax.sharding import PartitionSpec as P

MESH = pl.DeviceIdType.MESH
NODES = 4
BLOCK = 256
WIN = 64
NT = (((1,), (1,)), ((), ()))
VM = pl.BlockSpec(memory_space=pltpu.VMEM)
SM = pl.BlockSpec(memory_space=pltpu.SMEM)
F32, BF16, I32 = jnp.float32, jnp.bfloat16, jnp.int32


def iota(shape, dim, kind=I32):
    return lax.broadcasted_iota(I32, shape, dim).astype(kind)


def onehot(cond):
    return jnp.where(cond, 1.0, 0.0).astype(BF16)


def share_body(
    peers, cnt_s, g_ref, h_ref, idx_ref, node_ref, out_ref, ranks, offs, idx_v, node_v, send_sem, recv_sem, own_sem
):
    row, me = lax.axis_index("rows"), lax.axis_index("feat")
    lines = node_v.shape[0]
    slots = idx_v.shape[1]
    barrier = pltpu.get_barrier_semaphore()
    for d in range(1, peers):
        pl.semaphore_signal(barrier, inc=1, device_id=(row, lax.rem(me + d, peers)), device_id_type=MESH)
    own = [pltpu.make_async_copy(ref, out_ref.at[me, w], own_sem.at[w]) for w, ref in enumerate((g_ref, h_ref))]
    for c in own:
        c.start()
    fetch_idx = pltpu.make_async_copy(idx_ref, idx_v, own_sem.at[2])
    fetch_node = pltpu.make_async_copy(node_ref, node_v, own_sem.at[3])
    fetch_idx.start()
    fetch_node.start()
    count = cnt_s[0]
    for c in own:
        c.wait()
    pl.semaphore_wait(barrier, peers - 1)
    copies = []
    for d in range(1, peers):
        copies.append(
            pltpu.make_async_remote_copy(
                src_ref=out_ref.at[me],
                dst_ref=out_ref.at[me],
                send_sem=send_sem.at[d],
                recv_sem=recv_sem.at[d],
                device_id=(row, lax.rem(me + d, peers)),
                device_id_type=MESH,
            )
        )
    for c in copies:
        c.start()

    fetch_idx.wait()
    fetch_node.wait()
    node = node_v[...]
    kept = jnp.zeros((lines, 128), F32)
    for q in range(slots // 1024):
        ids = idx_v[:, pl.ds(q * 1024, 1024)]
        ids = jnp.where(iota((1, 1024), 1) + q * 1024 < count, ids, -1)
        upper = onehot(iota((lines, 1024), 0) == (ids >> 7))
        lower = onehot(iota((128, 1024), 0) == (ids & 127))
        kept += lax.dot_general(upper, lower, NT, preferred_element_type=F32)

    before = onehot(iota((128, 128), 0) < iota((128, 128), 1))
    above = onehot(iota((lines, lines), 1) < iota((lines, lines), 0))
    upto = onehot(iota((lines, 128), 0) < iota((lines, 128), 1))
    for k in range(NODES):
        mine = (kept > 0.5) & (node == k)
        ones = onehot(mine)
        per_line = jnp.sum(jnp.where(mine, 1.0, 0.0), axis=1, keepdims=True)
        rank = jnp.dot(ones, before, preferred_element_type=F32)
        rank += jnp.dot(above, jnp.broadcast_to(per_line, (lines, 128)).astype(BF16), preferred_element_type=F32)
        ranks[k] = jnp.where(mine, rank, -1.0)
        counts = lax.dot_general(jnp.ones((8, 128), BF16), ones, NT, preferred_element_type=F32)
        starts = jnp.dot(counts.astype(BF16), upto, preferred_element_type=F32)
        offs[pl.ds(k, 1), :] = starts[0:1].astype(I32)

    for c in copies:
        c.wait()


def share(kept_count, gradients, hessians, kept_index, node_ids, peers):
    part, slots, lines = gradients.shape[0], kept_index.shape[0], node_ids.shape[0] // 128
    hbm = pl.BlockSpec(memory_space=pltpu.HBM)
    big = [gradients.reshape(part // 128, 128), hessians.reshape(part // 128, 128), kept_index.reshape(1, slots), node_ids.reshape(lines, 128)]
    return pl.pallas_call(
        functools.partial(share_body, peers),
        out_shape=(
            jax.ShapeDtypeStruct((peers, 2, part // 128, 128), F32),
            jax.ShapeDtypeStruct((NODES, lines, 128), F32),
            jax.ShapeDtypeStruct((8, 128), I32),
        ),
        in_specs=[SM] + [hbm] * 4,
        out_specs=(VM, VM, VM),
        scratch_shapes=[pltpu.VMEM((1, slots), I32), pltpu.VMEM((lines, 128), I32)]
        + [pltpu.SemaphoreType.DMA(n) for n in ((peers,), (peers,), (4,))],
        compiler_params=pltpu.CompilerParams(collective_id=0, has_side_effects=True, vmem_limit_bytes=4 << 20),
        cost_estimate=pl.CostEstimate(flops=5_000_000_000, bytes_accessed=8_000_000, transcendentals=0),
        name="share",
    )(kept_count, *[pltpu.with_memory_space_constraint(v, pltpu.HBM) for v in big])


def hist_body(
    feat, gh, ranks, offs_v, flag_v, main_z, main_y, extra,
    xs, ws, pos, tpose, hi_a, lo_a, w16_a, hi_b, lo_b, w16_b, acc, exacc, totacc, offs_s, ext, osem,
):
    rows, width = feat.shape
    lines = rows // 128
    to_scalar = pltpu.make_async_copy(offs_v, offs_s, osem)
    to_scalar.start()

    factor = jnp.where(flag_v[...] == 1, 8.0, 1.0)
    grad = gh[:, 0].reshape(lines, 128) * factor
    hess = gh[:, 1].reshape(lines, 128) * factor
    tpose[...] = jnp.concatenate([grad, hess], axis=0).astype(BF16).astype(F32).T.astype(BF16)

    def clear(t, _):
        z = pl.multiple_of(t * 256, 256)
        xs[pl.ds(z, 256), :] = jnp.zeros((256, width), F32)
        ws[pl.ds(z, 256), :] = jnp.zeros((256, 128), F32)
        return 0

    lax.fori_loop(0, xs.shape[0] // 256, clear, 0)
    acc[...] = jnp.zeros_like(acc)
    exacc[...] = jnp.zeros_like(exacc)
    totacc[...] = jnp.zeros_like(totacc)
    to_scalar.wait()
    sizes = [offs_s[k, lines] for k in range(NODES)]
    bases, blocks = [], []
    base = jnp.int32(0)
    for k in range(NODES):
        bases.append(base)
        blocks.append((sizes[k] + (BLOCK - 1)) // BLOCK)
        base = base + blocks[k] * BLOCK
        rank = ranks[k]
        pos[k] = jnp.where(rank >= 0.0, rank + bases[k].astype(F32), -1.0)

    place = iota((WIN, 256), 0).astype(F32).astype(BF16)
    lane = iota((128, 128), 1) & (lines - 1)

    zero = jnp.zeros((), BF16)

    def line_of(t):
        r0 = pl.multiple_of(t * 256, 256)
        x = feat[pl.ds(r0, 256), :]
        tp = tpose[...]
        wn = jnp.concatenate([jnp.where(lane == 2 * t, tp, zero), jnp.where(lane == 2 * t + 1, tp, zero)], axis=0)
        first, trips = [], jnp.int32(1)
        for k in range(NODES):
            start = bases[k] + offs_s[k, 2 * t]
            stop = bases[k] + offs_s[k, 2 * t + 2]
            a = (start >> 3) << 3
            first.append(a)
            trips = jnp.maximum(trips, (stop - a + (WIN - 1)) >> 6)
        return x, wn, first, trips

    def window(t, i, x, wn, first):
        picks = []
        for k in range(NODES):
            pr = jnp.concatenate([pos[k, pl.ds(2 * t, 1), :], pos[k, pl.ds(2 * t + 1, 1), :]], axis=1)
            d = pr - (first[k] + WIN * i).astype(F32)
            d = jnp.where((d >= 0) & (d < WIN), d, -1.0)
            d = jnp.broadcast_to(d, (WIN, 256)).astype(BF16)
            picks.append(jnp.where(d == place, jnp.ones((), BF16), zero))
        pick = jnp.concatenate(picks, axis=0)
        got = jnp.dot(pick, x, preferred_element_type=F32)
        gotw = jnp.dot(pick, wn, preferred_element_type=F32)
        for k in range(NODES):
            at = pl.ds(pl.multiple_of(first[k] + WIN * i, 8), WIN)
            xs[at, :] += got[k * WIN:(k + 1) * WIN]
            ws[at, :] += gotw[k * WIN:(k + 1) * WIN]

    each = 8

    def compact(i, most):
        for u in range(each):
            x, wn, first, trips = line_of(i * each + u)
            window(i * each + u, 0, x, wn, first)
            most = jnp.maximum(most, trips)
        return most

    most = lax.fori_loop(0, rows // 256 // each, compact, jnp.int32(1))

    @pl.when(most > 1)
    def _():
        def more(t, _):
            x, wn, first, trips = line_of(t)

            def further(i, _):
                window(t, i, x, wn, first)
                return 0

            lax.fori_loop(1, trips, further, 0)
            return 0

        lax.fori_loop(0, rows // 256, more, 0)

    his = (iota((16, BLOCK), 0) & 7).astype(F32).astype(BF16)
    ramp = (iota((16, BLOCK), 0) + 1).astype(F32).astype(BF16)
    owner = iota((16, 256), 1) >> 4
    ends = [blocks[0], blocks[0] + blocks[1], blocks[0] + blocks[1] + blocks[2]]
    all_blocks = ends[2] + blocks[3]

    def node_at(q):
        return sum((q >= end).astype(I32) for end in ends)

    def prepare(q, hi_s, lo_s, w16_s):
        k = node_at(q)
        s = pl.multiple_of(q * BLOCK, BLOCK)
        x = xs[pl.ds(s, BLOCK), :]
        wt = ws[pl.ds(s, BLOCK), :].T
        w16 = jnp.concatenate(
            [jnp.broadcast_to(jnp.sum(wt[64 * w:64 * w + 64], axis=0, keepdims=True), (8, BLOCK)) for w in range(2)], axis=0
        )
        w16b = w16.astype(BF16)
        w16_s[...] = w16b
        totacc[k] += w16
        exacc[k] += jnp.dot(w16b, onehot(x <= 4.0), preferred_element_type=F32)
        cat = jnp.maximum(jnp.ceil(x.T * 16.0) + 64.0, 0.0)
        hi = jnp.floor(cat * 0.0625)
        hi_s[...] = hi
        lo_s[...] = cat - hi * 16.0 + 1.0

    def groups(q, hi_s, lo_s, w16_s):
        k = node_at(q)
        w16v = w16_s[...]
        for g in range(width // 16):
            f0 = (g >> 1) * 32 + (g & 1)
            a, b = [], []
            for f in range(16):
                hb = jnp.broadcast_to(hi_s[f0 + 2 * f:f0 + 2 * f + 1, :], (16, BLOCK)).astype(BF16)
                lb = jnp.broadcast_to(lo_s[f0 + 2 * f:f0 + 2 * f + 1, :], (16, BLOCK)).astype(BF16)
                a.append(jnp.where(hb == his, w16v, jnp.zeros((), BF16)))
                b.append(jnp.minimum(lb, ramp))
            r = lax.dot_general(jnp.concatenate(a, axis=0), jnp.concatenate(b, axis=0), NT, preferred_element_type=F32)
            mine = r[0:16]
            for f in range(1, 16):
                mine = jnp.where(owner == f, r[16 * f:16 * f + 16], mine)
            acc[k, g] += mine

    one, two = (hi_a, lo_a, w16_a), (hi_b, lo_b, w16_b)
    prepare(jnp.int32(0), *one)

    def blocks_of_two(i, _):
        q = 2 * i
        prepare(q + 1, *two)
        groups(q, *one)
        prepare(q + 2, *one)
        groups(q + 1, *two)
        return 0

    lax.fori_loop(0, all_blocks >> 1, blocks_of_two, 0)

    @pl.when((all_blocks & 1) == 1)
    def _():
        groups(all_blocks - 1, *one)

    r = iota((width, 128), 0) & 15
    for j in range(width // 32):
        parts = [acc[k, 2 * j + half, 8 * w:8 * w + 8, :] for half in range(2) for w in range(2) for k in range(NODES)]
        t = jnp.concatenate(parts, axis=0).T
        t = t - jnp.where(r == 0, 0.0, pltpu.roll(t, 1, 0))
        t = t - jnp.where(r == 15, 0.0, pltpu.roll(t, width - 1, 0))
        for z in range(8):
            for c in range(2):
                main_z[c, z, j] = t[(2 * z + c) * 16:(2 * z + c) * 16 + 8]
                main_y[c, j, z] = t[(2 * z + c) * 16 + 8:(2 * z + c) * 16 + 16]
    whole = [jnp.sum(totacc[k], axis=1, keepdims=True) for k in range(NODES)]
    lines_ex = [exacc[k, 8 * w:8 * w + 1, :] for w in range(2) for k in range(NODES)]
    lines_ex += [jnp.broadcast_to(whole[k][8 * w:8 * w + 1], (1, width)) for w in range(2) for k in range(NODES)]
    lines_ex.append(jnp.zeros((112, width), F32))
    ext[...] = jnp.concatenate(lines_ex, axis=0).T
    even, odd = ext[pl.ds(0, width // 2, stride=2), :], ext[pl.ds(1, width // 2, stride=2), :]
    both = even + pltpu.roll(odd, 16, 1)
    for j2 in range(2):
        packed = both[64 * j2:64 * j2 + 16]
        for i in range(1, 4):
            packed = packed + pltpu.roll(both[64 * j2 + 16 * i:64 * j2 + 16 * i + 16], 32 * i, 1)
        for z in range(8):
            for c in range(2):
                extra[c, z, j2:j2 + 1] = packed[2 * z + c:2 * z + c + 1]


def local_histogram(features, gh, ranks, offs, sample_flags, slots):
    rows, width = features.shape
    lines = rows // 128
    room = slots + NODES * BLOCK + 512
    return pl.pallas_call(
        hist_body,
        out_shape=(
            jax.ShapeDtypeStruct((2, 8, 8, 8, 128), F32),
            jax.ShapeDtypeStruct((2, 8, 8, 8, 128), F32),
            jax.ShapeDtypeStruct((2, 8, 2, 128), F32),
        ),
        in_specs=[VM] * 5,
        out_specs=(VM, VM, VM),
        scratch_shapes=[
            pltpu.VMEM((room, width), F32),
            pltpu.VMEM((room, 128), F32),
            pltpu.VMEM((NODES, lines, 128), F32),
            pltpu.VMEM((128, 128), BF16),
            pltpu.VMEM((width, BLOCK), F32),
            pltpu.VMEM((width, BLOCK), F32),
            pltpu.VMEM((16, BLOCK), BF16),
            pltpu.VMEM((width, BLOCK), F32),
            pltpu.VMEM((width, BLOCK), F32),
            pltpu.VMEM((16, BLOCK), BF16),
            pltpu.VMEM((NODES, width // 16, 16, 256), F32),
            pltpu.VMEM((NODES, 16, width), F32),
            pltpu.VMEM((NODES, 16, BLOCK), F32),
            pltpu.SMEM((8, 128), I32),
            pltpu.VMEM((width, 128), F32),
            pltpu.SemaphoreType.DMA,
        ],
        compiler_params=pltpu.CompilerParams(vmem_limit_bytes=30 << 20),
        name="local_histogram",
    )(
        features,
        gh,
        ranks,
        offs,
        sample_flags.reshape(lines, 128),
    )


FAR_FIRST = (4, 3, 5, 2, 6, 1, 7)
STEPS = 32000.0


def reduce_body(
    main_z, main_y, extra, edges, out,
    cz, cy, ce, qz, qy, fz, fy, rz, ry, gz, gy, uz, uy, ue, vz, vy, ve,
    sem1, sem2, sem3,
):
    row, feat = lax.axis_index("rows"), lax.axis_index("feat")
    core, z, y = lax.rem(row, 2), lax.rem(row // 2, 8), row // 16

    def at(yy, zz, cc):
        return (yy * 16 + zz * 2 + cc, feat)

    other = at(y, z, 1 - core)
    to_z = {d: at(y, lax.rem(z + d, 8), core) for d in FAR_FIRST}
    to_y = {d: at(lax.rem(y + d, 8), z, core) for d in FAR_FIRST}
    barrier = pltpu.get_barrier_semaphore()
    pl.semaphore_signal(barrier, inc=1, device_id=other, device_id_type=MESH)
    for d in FAR_FIRST:
        pl.semaphore_signal(barrier, inc=1, device_id=to_z[d], device_id_type=MESH)
        pl.semaphore_signal(barrier, inc=1, device_id=to_y[d], device_id_type=MESH)
    pl.semaphore_wait(barrier, 15)

    def copy(src, dst, sems, i, w, to):
        return pltpu.make_async_remote_copy(
            src_ref=src, dst_ref=dst, send_sem=sems.at[0, i, w], recv_sem=sems.at[1, i, w],
            device_id=to, device_id_type=MESH,
        )

    pair = {}
    for d in FAR_FIRST + (0,):
        zz, yy = lax.rem(z + d, 8), lax.rem(y + d, 8)
        pair[d] = (
            copy(main_z.at[1 - core, zz], cz.at[zz], sem1, d, 0, other),
            copy(main_y.at[1 - core, yy], cy.at[yy], sem1, d, 1, other),
            copy(extra.at[1 - core, zz], ce.at[zz], sem1, d, 2, other),
        )
        for c in pair[d]:
            c.start()

    def coded(v):
        v = v.reshape(64, 128)
        top = jnp.max(jnp.abs(v), axis=0, keepdims=True)
        q = jnp.floor(v * jnp.where(top > 0.0, STEPS / top, 0.0) + 0.5)
        return q.astype(I32).astype(jnp.int16), top * (1.0 / STEPS)

    def plain(q, step):
        return (q.astype(I32).astype(F32) * step).reshape(8, 8, 128)

    first = {}
    for d in FAR_FIRST + (0,):
        zz, yy = lax.rem(z + d, 8), lax.rem(y + d, 8)
        for c in pair[d]:
            c.wait_recv()
        sz = main_z[core, zz] + cz[zz]
        sy = main_y[core, yy] + cy[yy]
        se = extra[core, zz] + ce[zz]
        if d:
            qz[d - 1], step = coded(sz)
            fz[d - 1, 0:2] = se
            fz[d - 1, 2:3] = step
            qy[d - 1], step = coded(sy)
            fy[d - 1] = step
            first[d] = (
                copy(qz.at[d - 1], rz.at[d - 1], sem2, d - 1, 0, to_z[d]),
                copy(qy.at[d - 1], ry.at[d - 1], sem2, d - 1, 1, to_y[d]),
                copy(fz.at[d - 1], gz.at[d - 1], sem2, d - 1, 2, to_z[d]),
                copy(fy.at[d - 1], gy.at[d - 1], sem2, d - 1, 3, to_y[d]),
            )
            for c in first[d]:
                c.start()
    az, ay, ae = sz, sy, se
    for d in FAR_FIRST[::-1]:
        for c in first[d]:
            c.wait_recv()
        az += plain(rz[d - 1], gz[d - 1, 2:3])
        ay += plain(ry[d - 1], gy[d - 1])
        ae += gz[d - 1, 0:2]
    uz[...] = az
    uy[...] = ay
    ue[0] = ae[0:1]
    ue[1] = ae[1:2]

    second = {}
    for d in FAR_FIRST:
        zz, yy = lax.rem(z + d, 8), lax.rem(y + d, 8)
        second[d] = (
            copy(uz.at[yy], vz.at[d - 1], sem3, d - 1, 0, to_y[d]),
            copy(uy.at[zz], vy.at[d - 1], sem3, d - 1, 1, to_z[d]),
            copy(ue.at[yy // 4], ve.at[d - 1], sem3, d - 1, 2, to_y[d]),
        )
        for c in second[d]:
            c.start()
    a, b, e = uz[y], uy[z], ue[y // 4]
    for d in FAR_FIRST[::-1]:
        for c in second[d]:
            c.wait_recv()
        a += vz[d - 1]
        b += vy[d - 1]
        e += ve[d - 1]
    out[pl.ds(0, 8), :] = a
    out[pl.ds(8, 8), :] = b
    own = lax.rem(y, 4)
    for i in range(4):

        @pl.when(own == i)
        def _():
            out[pl.ds(16, 1), :] = pltpu.roll(jnp.broadcast_to(e, (8, 128)), (128 - 32 * i) % 128, 1)[0:1]

    out[pl.ds(17, 2), :] = edges[pl.ds(2 * row, 2), :].astype(F32)
    for c in [c for group in (pair, first, second) for some in group.values() for c in some]:
        c.wait_send()


def reduce_rows(main_z, main_y, extra, cut_edges):
    big, small = (8, 8, 8, 128), (8, 2, 128)
    coded = [pltpu.VMEM((7, 64, 128), jnp.int16)] * 2 + [pltpu.VMEM((7, 4, 128), F32), pltpu.VMEM((7, 1, 128), F32)]
    return pl.pallas_call(
        reduce_body,
        out_shape=jax.ShapeDtypeStruct((24, 128), F32),
        in_specs=[VM] * 4,
        out_specs=VM,
        scratch_shapes=[pltpu.VMEM(s, F32) for s in (big, big, small)]
        + coded
        + coded
        + [pltpu.VMEM(s, F32) for s in (big[1:], big[1:], (2, 1, 128))]
        + [pltpu.VMEM(s, F32) for s in ((7, 8, 128), (7, 8, 128), (7, 1, 128))]
        + [pltpu.SemaphoreType.DMA((2, n, m)) for n, m in ((8, 3), (7, 4), (7, 3))],
        compiler_params=pltpu.CompilerParams(collective_id=1, has_side_effects=True, vmem_limit_bytes=12 << 20),
        name="reduce_rows",
    )(main_z, main_y, extra, cut_edges)


def gain_body(sums, gain, rank):
    bins = sums[pl.ds(0, 16), :]
    b = sums[pl.ds(16, 1), :]
    hi = iota((16, 128), 1) & 7
    spread = jnp.concatenate([jnp.where(hi == h, bins, 0.0) for h in range(8)], axis=0)
    table = jnp.sum(spread.T.reshape(16, 8, 128), axis=1)
    column = jnp.broadcast_to(b, (128, 128)).T
    for half in range(2):
        e = sums[pl.ds(17 + half, 1), :]
        take = jnp.where(iota((128, 128), 0).astype(F32) <= e, 1.0, 0.0)
        left = lax.dot_general(
            table[half * 8:half * 8 + 8], take, (((1,), (0,)), ((), ())),
            precision=lax.Precision.HIGHEST, preferred_element_type=F32,
        )
        left = jnp.where(e >= 128.0, column[half * 16:half * 16 + 8], left)
        total = column[8:16]
        gl, hl, gs, hs = left[0:4], left[4:8], total[0:4], total[4:8]
        gain[half] = gl * gl / (hl + 1.0) + (gs - gl) * (gs - gl) / (hs - hl + 1.0) - gs * gs / (hs + 1.0)
        rank[half] = hl / hs


def gains(sums):
    out = jax.ShapeDtypeStruct((2, NODES, 128), F32)
    return pl.pallas_call(gain_body, out_shape=(out, out), in_specs=[VM], out_specs=(VM, VM), name="gains", compiler_params=pltpu.CompilerParams(vmem_limit_bytes=4 << 20))(sums)


def shards(features, gradients, hessians, node_ids, sample_flags, kept_index, kept_count, cut_edges):
    gh, ranks, offs = share(kept_count, gradients, hessians, kept_index, node_ids, lax.axis_size("feat"))
    main_z, main_y, extra = local_histogram(features, gh, ranks, offs, sample_flags, kept_index.shape[0])
    return gains(reduce_rows(main_z, main_y, extra, cut_edges))


def solution(mesh):
    placed = (
        P("rows", "feat"),
        P(("rows", "feat")),
        P(("rows", "feat")),
        P("rows"),
        P("rows"),
        P("rows"),
        P("rows"),
        P("feat", None),
    )
    return jax.shard_map(
        shards,
        mesh=mesh,
        in_specs=placed,
        out_specs=(P(("feat", "rows"), None, None), P(("feat", "rows"), None, None)),
        check_vma=False,
    )
```

```python
import functools

import jax
import jax.numpy as jnp
from jax import lax
from jax.experimental import pallas as pl
from jax.experimental.pallas import tpu as pltpu
from jax.sharding import PartitionSpec as P

MESH = pl.DeviceIdType.MESH
NODES = 4
BLOCK = 256
WIN = 64
NT = (((1,), (1,)), ((), ()))
VM = pl.BlockSpec(memory_space=pltpu.VMEM)
SM = pl.BlockSpec(memory_space=pltpu.SMEM)
F32, BF16, I32 = jnp.float32, jnp.bfloat16, jnp.int32


def iota(shape, dim, kind=I32):
    return lax.broadcasted_iota(I32, shape, dim).astype(kind)


def onehot(cond):
    return jnp.where(cond, 1.0, 0.0).astype(BF16)


def share_body(
    peers, cnt_s, g_ref, h_ref, idx_ref, node_ref, out_ref, ranks, offs, idx_v, node_v, send_sem, recv_sem, own_sem
):
    row, me = lax.axis_index("rows"), lax.axis_index("feat")
    lines = node_v.shape[0]
    slots = idx_v.shape[1]
    barrier = pltpu.get_barrier_semaphore()
    for d in range(1, peers):
        pl.semaphore_signal(barrier, inc=1, device_id=(row, lax.rem(me + d, peers)), device_id_type=MESH)
    own = [pltpu.make_async_copy(ref, out_ref.at[me, w], own_sem.at[w]) for w, ref in enumerate((g_ref, h_ref))]
    for c in own:
        c.start()
    fetch_idx = pltpu.make_async_copy(idx_ref, idx_v, own_sem.at[2])
    fetch_node = pltpu.make_async_copy(node_ref, node_v, own_sem.at[3])
    fetch_idx.start()
    fetch_node.start()
    count = cnt_s[0]
    for c in own:
        c.wait()
    pl.semaphore_wait(barrier, peers - 1)
    copies = []
    for d in range(1, peers):
        copies.append(
            pltpu.make_async_remote_copy(
                src_ref=out_ref.at[me],
                dst_ref=out_ref.at[me],
                send_sem=send_sem.at[d],
                recv_sem=recv_sem.at[d],
                device_id=(row, lax.rem(me + d, peers)),
                device_id_type=MESH,
            )
        )
    for c in copies:
        c.start()

    fetch_idx.wait()
    fetch_node.wait()
    node = node_v[...]
    kept = jnp.zeros((lines, 128), F32)
    for q in range(slots // 1024):
        ids = idx_v[:, pl.ds(q * 1024, 1024)]
        ids = jnp.where(iota((1, 1024), 1) + q * 1024 < count, ids, -1)
        upper = onehot(iota((lines, 1024), 0) == (ids >> 7))
        lower = onehot(iota((128, 1024), 0) == (ids & 127))
        kept += lax.dot_general(upper, lower, NT, preferred_element_type=F32)

    before = onehot(iota((128, 128), 0) < iota((128, 128), 1))
    above = onehot(iota((lines, lines), 1) < iota((lines, lines), 0))
    upto = onehot(iota((lines, 128), 0) < iota((lines, 128), 1))
    for k in range(NODES):
        mine = (kept > 0.5) & (node == k)
        ones = onehot(mine)
        per_line = jnp.sum(jnp.where(mine, 1.0, 0.0), axis=1, keepdims=True)
        rank = jnp.dot(ones, before, preferred_element_type=F32)
        rank += jnp.dot(above, jnp.broadcast_to(per_line, (lines, 128)).astype(BF16), preferred_element_type=F32)
        ranks[k] = jnp.where(mine, rank, -1.0)
        counts = lax.dot_general(jnp.ones((8, 128), BF16), ones, NT, preferred_element_type=F32)
        starts = jnp.dot(counts.astype(BF16), upto, preferred_element_type=F32)
        offs[pl.ds(k, 1), :] = starts[0:1].astype(I32)

    for c in copies:
        c.wait()


def share(kept_count, gradients, hessians, kept_index, node_ids, peers):
    part, slots, lines = gradients.shape[0], kept_index.shape[0], node_ids.shape[0] // 128
    hbm = pl.BlockSpec(memory_space=pltpu.HBM)
    big = [gradients.reshape(part // 128, 128), hessians.reshape(part // 128, 128), kept_index.reshape(1, slots), node_ids.reshape(lines, 128)]
    return pl.pallas_call(
        functools.partial(share_body, peers),
        out_shape=(
            jax.ShapeDtypeStruct((peers, 2, part // 128, 128), F32),
            jax.ShapeDtypeStruct((NODES, lines, 128), F32),
            jax.ShapeDtypeStruct((8, 128), I32),
        ),
        in_specs=[SM] + [hbm] * 4,
        out_specs=(VM, VM, VM),
        scratch_shapes=[pltpu.VMEM((1, slots), I32), pltpu.VMEM((lines, 128), I32)]
        + [pltpu.SemaphoreType.DMA(n) for n in ((peers,), (peers,), (4,))],
        compiler_params=pltpu.CompilerParams(collective_id=0, has_side_effects=True, vmem_limit_bytes=4 << 20),
        cost_estimate=pl.CostEstimate(flops=5_000_000_000, bytes_accessed=8_000_000, transcendentals=0),
        name="share",
    )(kept_count, *[pltpu.with_memory_space_constraint(v, pltpu.HBM) for v in big])


def hist_body(
    feat, gh, ranks, offs_v, flag_v, main_z, main_y, extra,
    xs, ws, pos, tpose, hi_a, lo_a, w16_a, hi_b, lo_b, w16_b, acc, exacc, totacc, offs_s, ext, osem,
):
    rows, width = feat.shape
    lines = rows // 128
    to_scalar = pltpu.make_async_copy(offs_v, offs_s, osem)
    to_scalar.start()

    factor = jnp.where(flag_v[...] == 1, 8.0, 1.0)
    grad = gh[:, 0].reshape(lines, 128) * factor
    hess = gh[:, 1].reshape(lines, 128) * factor
    tpose[...] = jnp.concatenate([grad, hess], axis=0).astype(BF16).astype(F32).T.astype(BF16)

    def clear(t, _):
        z = pl.multiple_of(t * 256, 256)
        xs[pl.ds(z, 256), :] = jnp.zeros((256, width), F32)
        ws[pl.ds(z, 256), :] = jnp.zeros((256, 128), F32)
        return 0

    lax.fori_loop(0, xs.shape[0] // 256, clear, 0)
    acc[...] = jnp.zeros_like(acc)
    exacc[...] = jnp.zeros_like(exacc)
    totacc[...] = jnp.zeros_like(totacc)
    to_scalar.wait()
    sizes = [offs_s[k, lines] for k in range(NODES)]
    bases, blocks = [], []
    base = jnp.int32(0)
    for k in range(NODES):
        bases.append(base)
        blocks.append((sizes[k] + (BLOCK - 1)) // BLOCK)
        base = base + blocks[k] * BLOCK
        rank = ranks[k]
        pos[k] = jnp.where(rank >= 0.0, rank + bases[k].astype(F32), -1.0)

    place = iota((WIN, 256), 0).astype(F32).astype(BF16)
    lane = iota((128, 128), 1) & (lines - 1)

    zero = jnp.zeros((), BF16)

    def line_of(t):
        r0 = pl.multiple_of(t * 256, 256)
        x = feat[pl.ds(r0, 256), :]
        tp = tpose[...]
        wn = jnp.concatenate([jnp.where(lane == 2 * t, tp, zero), jnp.where(lane == 2 * t + 1, tp, zero)], axis=0)
        first, trips = [], jnp.int32(1)
        for k in range(NODES):
            start = bases[k] + offs_s[k, 2 * t]
            stop = bases[k] + offs_s[k, 2 * t + 2]
            a = (start >> 3) << 3
            first.append(a)
            trips = jnp.maximum(trips, (stop - a + (WIN - 1)) >> 6)
        return x, wn, first, trips

    def window(t, i, x, wn, first):
        picks = []
        for k in range(NODES):
            pr = jnp.concatenate([pos[k, pl.ds(2 * t, 1), :], pos[k, pl.ds(2 * t + 1, 1), :]], axis=1)
            d = pr - (first[k] + WIN * i).astype(F32)
            d = jnp.where((d >= 0) & (d < WIN), d, -1.0)
            d = jnp.broadcast_to(d, (WIN, 256)).astype(BF16)
            picks.append(jnp.where(d == place, jnp.ones((), BF16), zero))
        pick = jnp.concatenate(picks, axis=0)
        got = jnp.dot(pick, x, preferred_element_type=F32)
        gotw = jnp.dot(pick, wn, preferred_element_type=F32)
        for k in range(NODES):
            at = pl.ds(pl.multiple_of(first[k] + WIN * i, 8), WIN)
            xs[at, :] += got[k * WIN:(k + 1) * WIN]
            ws[at, :] += gotw[k * WIN:(k + 1) * WIN]

    each = 16

    def compact(i, most):
        for u in range(each):
            x, wn, first, trips = line_of(i * each + u)
            window(i * each + u, 0, x, wn, first)
            most = jnp.maximum(most, trips)
        return most

    most = lax.fori_loop(0, rows // 256 // each, compact, jnp.int32(1))

    @pl.when(most > 1)
    def _():
        def more(t, _):
            x, wn, first, trips = line_of(t)

            def further(i, _):
                window(t, i, x, wn, first)
                return 0

            lax.fori_loop(1, trips, further, 0)
            return 0

        lax.fori_loop(0, rows // 256, more, 0)

    his = (iota((16, BLOCK), 0) & 7).astype(F32).astype(BF16)
    ramp = (iota((16, BLOCK), 0) + 1).astype(F32).astype(BF16)
    owner = iota((16, 256), 1) >> 4
    ends = [blocks[0], blocks[0] + blocks[1], blocks[0] + blocks[1] + blocks[2]]
    all_blocks = ends[2] + blocks[3]

    def node_at(q):
        return sum((q >= end).astype(I32) for end in ends)

    def prepare(q, hi_s, lo_s, w16_s):
        k = node_at(q)
        s = pl.multiple_of(q * BLOCK, BLOCK)
        x = xs[pl.ds(s, BLOCK), :]
        wt = ws[pl.ds(s, BLOCK), :].T
        w16 = jnp.concatenate(
            [jnp.broadcast_to(jnp.sum(wt[64 * w:64 * w + 64], axis=0, keepdims=True), (8, BLOCK)) for w in range(2)], axis=0
        )
        w16b = w16.astype(BF16)
        w16_s[...] = w16b
        totacc[k] += w16
        exacc[k] += jnp.dot(w16b, onehot(x <= 4.0), preferred_element_type=F32)
        cat = jnp.maximum(jnp.ceil(x.T * 16.0) + 64.0, 0.0)
        hi = jnp.floor(cat * 0.0625)
        hi_s[...] = hi
        lo_s[...] = cat - hi * 16.0 + 1.0

    def groups(q, hi_s, lo_s, w16_s):
        k = node_at(q)
        w16v = w16_s[...]
        for g in range(width // 16):
            f0 = (g >> 1) * 32 + (g & 1)
            a, b = [], []
            for f in range(16):
                hb = jnp.broadcast_to(hi_s[f0 + 2 * f:f0 + 2 * f + 1, :], (16, BLOCK)).astype(BF16)
                lb = jnp.broadcast_to(lo_s[f0 + 2 * f:f0 + 2 * f + 1, :], (16, BLOCK)).astype(BF16)
                a.append(jnp.where(hb == his, w16v, jnp.zeros((), BF16)))
                b.append(jnp.minimum(lb, ramp))
            r = lax.dot_general(jnp.concatenate(a, axis=0), jnp.concatenate(b, axis=0), NT, preferred_element_type=F32)
            mine = r[0:16]
            for f in range(1, 16):
                mine = jnp.where(owner == f, r[16 * f:16 * f + 16], mine)
            acc[k, g] += mine

    one, two = (hi_a, lo_a, w16_a), (hi_b, lo_b, w16_b)
    prepare(jnp.int32(0), *one)

    def blocks_of_two(i, _):
        q = 2 * i
        prepare(q + 1, *two)
        groups(q, *one)
        prepare(q + 2, *one)
        groups(q + 1, *two)
        return 0

    lax.fori_loop(0, all_blocks >> 1, blocks_of_two, 0)

    @pl.when((all_blocks & 1) == 1)
    def _():
        groups(all_blocks - 1, *one)

    r = iota((width, 128), 0) & 15
    for j in range(width // 32):
        parts = [acc[k, 2 * j + half, 8 * w:8 * w + 8, :] for half in range(2) for w in range(2) for k in range(NODES)]
        t = jnp.concatenate(parts, axis=0).T
        t = t - jnp.where(r == 0, 0.0, pltpu.roll(t, 1, 0))
        t = t - jnp.where(r == 15, 0.0, pltpu.roll(t, width - 1, 0))
        for z in range(8):
            for c in range(2):
                main_z[c, z, j] = t[(2 * z + c) * 16:(2 * z + c) * 16 + 8]
                main_y[c, j, z] = t[(2 * z + c) * 16 + 8:(2 * z + c) * 16 + 16]
    whole = [jnp.sum(totacc[k], axis=1, keepdims=True) for k in range(NODES)]
    lines_ex = [exacc[k, 8 * w:8 * w + 1, :] for w in range(2) for k in range(NODES)]
    lines_ex += [jnp.broadcast_to(whole[k][8 * w:8 * w + 1], (1, width)) for w in range(2) for k in range(NODES)]
    lines_ex.append(jnp.zeros((112, width), F32))
    ext[...] = jnp.concatenate(lines_ex, axis=0).T
    even, odd = ext[pl.ds(0, width // 2, stride=2), :], ext[pl.ds(1, width // 2, stride=2), :]
    both = even + pltpu.roll(odd, 16, 1)
    for j2 in range(2):
        packed = both[64 * j2:64 * j2 + 16]
        for i in range(1, 4):
            packed = packed + pltpu.roll(both[64 * j2 + 16 * i:64 * j2 + 16 * i + 16], 32 * i, 1)
        for z in range(8):
            for c in range(2):
                extra[c, z, j2:j2 + 1] = packed[2 * z + c:2 * z + c + 1]


def local_histogram(features, gh, ranks, offs, sample_flags, slots):
    rows, width = features.shape
    lines = rows // 128
    room = slots + NODES * BLOCK + 512
    return pl.pallas_call(
        hist_body,
        out_shape=(
            jax.ShapeDtypeStruct((2, 8, 8, 8, 128), F32),
            jax.ShapeDtypeStruct((2, 8, 8, 8, 128), F32),
            jax.ShapeDtypeStruct((2, 8, 2, 128), F32),
        ),
        in_specs=[VM] * 5,
        out_specs=(VM, VM, VM),
        scratch_shapes=[
            pltpu.VMEM((room, width), F32),
            pltpu.VMEM((room, 128), F32),
            pltpu.VMEM((NODES, lines, 128), F32),
            pltpu.VMEM((128, 128), BF16),
            pltpu.VMEM((width, BLOCK), F32),
            pltpu.VMEM((width, BLOCK), F32),
            pltpu.VMEM((16, BLOCK), BF16),
            pltpu.VMEM((width, BLOCK), F32),
            pltpu.VMEM((width, BLOCK), F32),
            pltpu.VMEM((16, BLOCK), BF16),
            pltpu.VMEM((NODES, width // 16, 16, 256), F32),
            pltpu.VMEM((NODES, 16, width), F32),
            pltpu.VMEM((NODES, 16, BLOCK), F32),
            pltpu.SMEM((8, 128), I32),
            pltpu.VMEM((width, 128), F32),
            pltpu.SemaphoreType.DMA,
        ],
        compiler_params=pltpu.CompilerParams(vmem_limit_bytes=30 << 20),
        name="local_histogram",
    )(
        features,
        gh,
        ranks,
        offs,
        sample_flags.reshape(lines, 128),
    )


FAR_FIRST = (4, 3, 5, 2, 6, 1, 7)
STEPS = 32000.0


def reduce_body(
    main_z, main_y, extra, edges, out,
    cz, cy, ce, qz, qy, fz, fy, rz, ry, gz, gy, uz, uy, ue, vz, vy, ve,
    sem1, sem2, sem3,
):
    row, feat = lax.axis_index("rows"), lax.axis_index("feat")
    core, z, y = lax.rem(row, 2), lax.rem(row // 2, 8), row // 16

    def at(yy, zz, cc):
        return (yy * 16 + zz * 2 + cc, feat)

    other = at(y, z, 1 - core)
    to_z = {d: at(y, lax.rem(z + d, 8), core) for d in FAR_FIRST}
    to_y = {d: at(lax.rem(y + d, 8), z, core) for d in FAR_FIRST}
    barrier = pltpu.get_barrier_semaphore()
    pl.semaphore_signal(barrier, inc=1, device_id=other, device_id_type=MESH)
    for d in FAR_FIRST:
        pl.semaphore_signal(barrier, inc=1, device_id=to_z[d], device_id_type=MESH)
        pl.semaphore_signal(barrier, inc=1, device_id=to_y[d], device_id_type=MESH)
    pl.semaphore_wait(barrier, 15)

    def copy(src, dst, sems, i, w, to):
        return pltpu.make_async_remote_copy(
            src_ref=src, dst_ref=dst, send_sem=sems.at[0, i, w], recv_sem=sems.at[1, i, w],
            device_id=to, device_id_type=MESH,
        )

    pair = {}
    for d in FAR_FIRST + (0,):
        zz, yy = lax.rem(z + d, 8), lax.rem(y + d, 8)
        pair[d] = (
            copy(main_z.at[1 - core, zz], cz.at[zz], sem1, d, 0, other),
            copy(main_y.at[1 - core, yy], cy.at[yy], sem1, d, 1, other),
            copy(extra.at[1 - core, zz], ce.at[zz], sem1, d, 2, other),
        )
        for c in pair[d]:
            c.start()

    def coded(v):
        v = v.reshape(64, 128)
        top = jnp.max(jnp.abs(v), axis=0, keepdims=True)
        q = jnp.floor(v * jnp.where(top > 0.0, STEPS / top, 0.0) + 0.5)
        return q.astype(I32).astype(jnp.int16), top * (1.0 / STEPS)

    def plain(q, step):
        return (q.astype(I32).astype(F32) * step).reshape(8, 8, 128)

    first = {}
    for d in FAR_FIRST + (0,):
        zz, yy = lax.rem(z + d, 8), lax.rem(y + d, 8)
        for c in pair[d]:
            c.wait_recv()
        sz = main_z[core, zz] + cz[zz]
        sy = main_y[core, yy] + cy[yy]
        se = extra[core, zz] + ce[zz]
        if d:
            qz[d - 1], step = coded(sz)
            fz[d - 1, 0:2] = se
            fz[d - 1, 2:3] = step
            qy[d - 1], step = coded(sy)
            fy[d - 1] = step
            first[d] = (
                copy(qz.at[d - 1], rz.at[d - 1], sem2, d - 1, 0, to_z[d]),
                copy(qy.at[d - 1], ry.at[d - 1], sem2, d - 1, 1, to_y[d]),
                copy(fz.at[d - 1], gz.at[d - 1], sem2, d - 1, 2, to_z[d]),
                copy(fy.at[d - 1], gy.at[d - 1], sem2, d - 1, 3, to_y[d]),
            )
            for c in first[d]:
                c.start()
    az, ay, ae = sz, sy, se
    for d in FAR_FIRST[::-1]:
        for c in first[d]:
            c.wait_recv()
        az += plain(rz[d - 1], gz[d - 1, 2:3])
        ay += plain(ry[d - 1], gy[d - 1])
        ae += gz[d - 1, 0:2]
    uz[...] = az
    uy[...] = ay
    ue[0] = ae[0:1]
    ue[1] = ae[1:2]

    second = {}
    for d in FAR_FIRST:
        zz, yy = lax.rem(z + d, 8), lax.rem(y + d, 8)
        second[d] = (
            copy(uz.at[yy], vz.at[d - 1], sem3, d - 1, 0, to_y[d]),
            copy(uy.at[zz], vy.at[d - 1], sem3, d - 1, 1, to_z[d]),
            copy(ue.at[yy // 4], ve.at[d - 1], sem3, d - 1, 2, to_y[d]),
        )
        for c in second[d]:
            c.start()
    a, b, e = uz[y], uy[z], ue[y // 4]
    for d in FAR_FIRST[::-1]:
        for c in second[d]:
            c.wait_recv()
        a += vz[d - 1]
        b += vy[d - 1]
        e += ve[d - 1]
    out[pl.ds(0, 8), :] = a
    out[pl.ds(8, 8), :] = b
    own = lax.rem(y, 4)
    for i in range(4):

        @pl.when(own == i)
        def _():
            out[pl.ds(16, 1), :] = pltpu.roll(jnp.broadcast_to(e, (8, 128)), (128 - 32 * i) % 128, 1)[0:1]

    out[pl.ds(17, 2), :] = edges[pl.ds(2 * row, 2), :].astype(F32)
    for c in [c for group in (pair, first, second) for some in group.values() for c in some]:
        c.wait_send()


def reduce_rows(main_z, main_y, extra, cut_edges):
    big, small = (8, 8, 8, 128), (8, 2, 128)
    coded = [pltpu.VMEM((7, 64, 128), jnp.int16)] * 2 + [pltpu.VMEM((7, 4, 128), F32), pltpu.VMEM((7, 1, 128), F32)]
    return pl.pallas_call(
        reduce_body,
        out_shape=jax.ShapeDtypeStruct((24, 128), F32),
        in_specs=[VM] * 4,
        out_specs=VM,
        scratch_shapes=[pltpu.VMEM(s, F32) for s in (big, big, small)]
        + coded
        + coded
        + [pltpu.VMEM(s, F32) for s in (big[1:], big[1:], (2, 1, 128))]
        + [pltpu.VMEM(s, F32) for s in ((7, 8, 128), (7, 8, 128), (7, 1, 128))]
        + [pltpu.SemaphoreType.DMA((2, n, m)) for n, m in ((8, 3), (7, 4), (7, 3))],
        compiler_params=pltpu.CompilerParams(collective_id=1, has_side_effects=True, vmem_limit_bytes=12 << 20),
        name="reduce_rows",
    )(main_z, main_y, extra, cut_edges)


def gain_body(sums, gain, rank):
    bins = sums[pl.ds(0, 16), :]
    b = sums[pl.ds(16, 1), :]
    hi = iota((16, 128), 1) & 7
    spread = jnp.concatenate([jnp.where(hi == h, bins, 0.0) for h in range(8)], axis=0)
    table = jnp.sum(spread.T.reshape(16, 8, 128), axis=1)
    column = jnp.broadcast_to(b, (128, 128)).T
    pieces = []
    for half in range(2):
        rest, parts = table[half * 8:half * 8 + 8], []
        for _ in range(3):
            parts.append(rest.astype(BF16).astype(F32))
            rest = rest - parts[-1]
        pieces.append(jnp.concatenate(parts, axis=0).astype(BF16))
    for half in range(2):
        e = sums[pl.ds(17 + half, 1), :]
        take = onehot(iota((128, 128), 0).astype(F32) <= e)
        three = jnp.dot(pieces[half], take, preferred_element_type=F32)
        left = three[0:8] + three[8:16] + three[16:24]
        left = jnp.where(e >= 128.0, column[half * 16:half * 16 + 8], left)
        total = column[8:16]
        gl, hl, gs, hs = left[0:4], left[4:8], total[0:4], total[4:8]
        gain[half] = gl * gl / (hl + 1.0) + (gs - gl) * (gs - gl) / (hs - hl + 1.0) - gs * gs / (hs + 1.0)
        rank[half] = hl / hs


def gains(sums):
    out = jax.ShapeDtypeStruct((2, NODES, 128), F32)
    return pl.pallas_call(gain_body, out_shape=(out, out), in_specs=[VM], out_specs=(VM, VM), name="gains", compiler_params=pltpu.CompilerParams(vmem_limit_bytes=4 << 20))(sums)


def shards(features, gradients, hessians, node_ids, sample_flags, kept_index, kept_count, cut_edges):
    gh, ranks, offs = share(kept_count, gradients, hessians, kept_index, node_ids, lax.axis_size("feat"))
    main_z, main_y, extra = local_histogram(features, gh, ranks, offs, sample_flags, kept_index.shape[0])
    return gains(reduce_rows(main_z, main_y, extra, cut_edges))


def solution(mesh):
    placed = (
        P("rows", "feat"),
        P(("rows", "feat")),
        P(("rows", "feat")),
        P("rows"),
        P("rows"),
        P("rows"),
        P("rows"),
        P("feat", None),
    )
    return jax.shard_map(
        shards,
        mesh=mesh,
        in_specs=placed,
        out_specs=(P(("feat", "rows"), None, None), P(("feat", "rows"), None, None)),
        check_vma=False,
    )
```
